32 devices in a mesh: grp: 2 (over y), row: 8 (over z, x), col: 2 (over core).
Axes of the slice: x: 2, y: 2, z: 4, core: 2. Of those that a mesh axis runs over, the one named last changes fastest.
Arguments:
- normed_features: bfloat16 [64, 32, 256], P(('grp', 'col'), 'row'), parts along dimension 0, may hold values from -6 to 6
- alignment_mask: int32 [64, 32], P(('grp', 'col'), 'row'), parts along dimension 0, may hold values from 0 to 1, as said below
- residue_present_mask: int32 [64], P(('grp', 'row')), parts along dimension 0, may hold values from 0 to 1
- first_factor_matrix: bfloat16 [256, 32], replicated, may hold values from -0.375 to 0.375
- second_factor_matrix: bfloat16 [256, 32], replicated, may hold values from -0.375 to 0.375
- output_weight: bfloat16 [1024, 128], replicated, may hold values from -0.75 to 0.75
- pairwise_bias: float32 [128], replicated, may hold values from -3 to 3
- cotangent: bfloat16 [64, 32, 128], P(('grp', 'row'), 'col'), parts along dimension 0, may hold values from -0.72 to 0.72
Outputs:
- pair_update: bfloat16 [64, 32, 128], P(('grp', 'row'), 'col'), parts along dimension 0
- left_grad: float32 [64, 32, 32], P(('grp', 'col'), 'row'), parts along dimension 0
- right_grad: float32 [64, 32, 32], P(('grp', 'col'), 'row'), parts along dimension 0
The draws below stay inside these ranges and needn't reach their ends.
There are 2 independent parts, one for each index of `grp`. The reference program is written for one: setup_inputs(seed, part) draws one part's arguments, and reference() takes and returns one part's arrays. A program takes and returns all parts, laid end to end along the dimension named above; an argument that names none is the same for every part. Nothing has to cross between parts.
Inputs may be any that keep to these rules, and one draw needn't show every extreme that they name: `alignment_mask`: 0 or 1; sequence 0 (the query) is present at every residue.
All inputs are finite; a program needn't handle non-finite values.
Results may differ from the reference program's by a relative error of at most 0.006.
Values may be sent and summed in bfloat16 or wider, within the bound.
A program may use at most 64 MiB of HBM per device.

```python
import math
import jax
import jax.numpy as jnp
from jax import lax

FEATURE_DEPTH = 256
PROJ_DEPTH = 32
CZ = 128
RES_DEV = 4
ALIGNED_CHAINS = 32
CUT_POSITIONS = 32


def draw_alignment_mask(key, part):
    chain_number = jnp.arange(ALIGNED_CHAINS, dtype=jnp.int32)[:, None]
    upper_cap = 30 + 65 * chain_number // max(ALIGNED_CHAINS - 1, 1)
    cyclic_shifted = jax.random.randint(jax.random.fold_in(key, 17), (ALIGNED_CHAINS, CUT_POSITIONS), 0, 100, dtype=jnp.int32)
    present = (cyclic_shifted < upper_cap).astype(jnp.int32)
    return jnp.where(chain_number == 0, 1, present).astype(jnp.int32)


def present_residues(key):
    picks = jax.random.randint(jax.random.fold_in(key, 29), (CUT_POSITIONS,), 0, 8, dtype=jnp.int32)
    return (picks < 7).astype(jnp.int32)


def draw_residue_present_mask(key, part):
    return present_residues(key)


def draw_cotangent(key, part):
    present = present_residues(key).astype(jnp.float32)
    noise_key = jax.random.fold_in(key, 41)
    shape = (CUT_POSITIONS, CUT_POSITIONS, CZ)
    base = jnp.clip(jax.random.normal(noise_key, shape, jnp.float32), -6.0, 6.0)
    block_order = jax.random.permutation(jax.random.fold_in(key, 53), CUT_POSITIONS // RES_DEV)
    block_number = jnp.arange(CUT_POSITIONS, dtype=jnp.int32) // RES_DEV
    paired = block_order[block_number][:, None] == block_number[None, :]
    boost = jnp.where(paired, 4.0, 1.0)
    pair_live = present[:, None] * present[None, :]
    weight = boost * (0.08 + 0.92 * pair_live)
    return (0.03 * base * weight[:, :, None]).astype(jnp.bfloat16)


def shard_levels(own_key, shape, pieces, least, high):
    loudness, own = 1.0, jax.random.fold_in(own_key, 6)
    for axis_at, shards_of in pieces:
        heights = jnp.exp(jax.random.uniform(jax.random.fold_in(own, axis_at), (shards_of,), jnp.float32, least / len(pieces), high / len(pieces)))
        loudness = loudness * jnp.repeat(heights, shape[axis_at] // shards_of).reshape([-1 if axis == axis_at else 1 for axis in range(len(shape))])
    return loudness


def centred(own_key, shape, width, most, shards=(), held_as=jnp.bfloat16):
    array = jax.random.normal(own_key, shape, jnp.float32) * width
    if len(shards) > 0:
        array = shard_levels(own_key, shape, shards, -0.22, 0.18) * array
    return jnp.clip(array, min=-most, max=most).astype(held_as)


def setup_inputs(seed: int = 0, part: int = 0) -> dict:
    seeds = jax.random.split(jax.random.key(seed), 9)
    part_splits = jax.random.split(jax.random.fold_in(seeds[8], part), 9)
    normed_features = centred(part_splits[0], (ALIGNED_CHAINS, CUT_POSITIONS, FEATURE_DEPTH), 1.0, 6.0, ((0, 2), (1, 8)))
    alignment_mask = draw_alignment_mask(jax.random.fold_in(jax.random.fold_in(seeds[8], part), 71), part)
    residue_present_mask = draw_residue_present_mask(jax.random.fold_in(jax.random.fold_in(seeds[8], part), 71), part)
    first_factor_matrix = centred(seeds[3], (FEATURE_DEPTH, PROJ_DEPTH), FEATURE_DEPTH ** -0.5, 0.375)
    second_factor_matrix = centred(seeds[4], (FEATURE_DEPTH, PROJ_DEPTH), FEATURE_DEPTH ** -0.5, 0.375)
    output_weight = centred(seeds[5], (PROJ_DEPTH * PROJ_DEPTH, CZ), (PROJ_DEPTH * PROJ_DEPTH // 16) ** -0.5, 0.75)
    pairwise_bias = centred(seeds[6], (CZ,), 0.5, 3.0, (), jnp.float32)
    cotangent = draw_cotangent(jax.random.fold_in(jax.random.fold_in(seeds[8], part), 71), part)
    return {"normed_features": normed_features, "alignment_mask": alignment_mask, "residue_present_mask": residue_present_mask, "first_factor_matrix": first_factor_matrix, "second_factor_matrix": second_factor_matrix, "output_weight": output_weight, "pairwise_bias": pairwise_bias, "cotangent": cotangent}


def reference(normed_features, alignment_mask, residue_present_mask, first_factor_matrix, second_factor_matrix, output_weight, pairwise_bias, cotangent):
    sequence_count = normed_features.shape[0]
    residue_count = normed_features.shape[1]
    proj_width = first_factor_matrix.shape[1]
    channels = output_weight.shape[1]
    present_entry_mask = alignment_mask.astype(jnp.float32) * residue_present_mask.astype(jnp.float32)[None, :]
    activation_broad = normed_features.astype(jnp.float32)
    left_proj = (jnp.einsum("srk,kc->src", activation_broad, first_factor_matrix.astype(jnp.float32)) * present_entry_mask[:, :, None]).astype(jnp.bfloat16)
    right_proj = (jnp.einsum("srk,kc->src", activation_broad, second_factor_matrix.astype(jnp.float32)) * present_entry_mask[:, :, None]).astype(jnp.bfloat16)
    pair_count = jnp.dot(present_entry_mask.T, present_entry_mask, precision=lax.Precision.HIGHEST)
    divisor = jnp.maximum(pair_count, 1.0)
    row_block = math.gcd(residue_count, 32)
    num_blocks = residue_count // row_block
    right_wide = right_proj.astype(jnp.float32)

    def per_block(running, block_idx):
        offset = (block_idx * row_block).astype(jnp.int32)
        left_blk = lax.dynamic_slice_in_dim(left_proj, offset, row_block, 1).astype(jnp.float32)
        div_blk = lax.dynamic_slice_in_dim(divisor, offset, row_block, 0)
        cot_blk = lax.dynamic_slice_in_dim(cotangent, offset, row_block, 0)
        products = jnp.einsum("sic,sje->ijce", left_blk, right_wide).astype(jnp.bfloat16)
        products = products.reshape(row_block * residue_count, proj_width * proj_width)
        mapped = jnp.dot(products, output_weight, preferred_element_type=jnp.float32).reshape(row_block, residue_count, channels)
        pair_blk = (mapped / div_blk[:, :, None] + pairwise_bias[None, None, :]).astype(jnp.bfloat16)
        scaled = (cot_blk.astype(jnp.float32) / div_blk[:, :, None]).astype(jnp.bfloat16).reshape(row_block * residue_count, channels)
        grad_outer = jnp.dot(scaled, output_weight.T, preferred_element_type=jnp.float32).astype(jnp.bfloat16)
        grad_outer = grad_outer.reshape(row_block, residue_count, proj_width, proj_width).astype(jnp.float32)
        left_term = jnp.einsum("ijce,sje->sic", grad_outer, right_wide)
        right_term = jnp.einsum("ijce,sic->sje", grad_outer, left_blk)
        return running + right_term, (pair_blk, left_term)

    start_grad = jnp.zeros((sequence_count, residue_count, proj_width), jnp.float32)
    right_grad, (pairs, left_terms) = lax.scan(per_block, start_grad, jnp.arange(num_blocks, dtype=jnp.int32))
    pair_update = pairs.reshape(residue_count, residue_count, channels)
    left_grad = jnp.moveaxis(left_terms, 0, 1).reshape(sequence_count, residue_count, proj_width)
    return pair_update, left_grad, right_grad
```

```python
import functools

import jax
import jax.numpy as jnp
from jax import lax
from jax.experimental import pallas as pl
from jax.experimental.pallas import tpu as pltpu
from jax.sharding import PartitionSpec as P

F32 = jnp.float32
BF16 = jnp.bfloat16
MESH = pl.DeviceIdType.MESH
UNROLL = 8
GRANT = 40 << 20


def iota(shape, axis):
    return lax.broadcasted_iota(jnp.int32, shape, axis)


def mm(a, b):
    return lax.dot_general(a, b, (((1,), (0,)), ((), ())), preferred_element_type=F32)


def mm_t(a, b):
    return lax.dot_general(a, b, (((1,), (1,)), ((), ())), preferred_element_type=F32)


def each(n, f):
    if n <= UNROLL:
        for k in range(n):
            f(k)
    else:

        @pl.loop(0, n)
        def _(k):
            f(k)


def block_rows(nrow):
    n = min(nrow, 8)
    while nrow % n:
        n -= 1
    return n


def kernel(
    nrow,
    x_hbm, am_hbm, rm_hbm, wl_hbm, wr_hbm, w_hbm, bias_hbm, cot_hbm,
    pu_ref, lg_ref, rg_ref,
    x_ref, am_ref, rm_ref, wl_ref, wr_ref, w_ref, bias_ref, cot_ref,
    g_s, g_r, n_s, n_r, f_s, f_r, ct_s, ct_r, cf_r, m_s, m_r,
    w32, a32, c32, c32b, inv_ref, og_a, og_b, wt_ref, p2,
    ssem, rsem, psem, isem,
):
    seq, loc, feat = x_ref.shape
    proj = wl_ref.shape[0]
    half_res, chan = cot_ref.shape[1], cot_ref.shape[2]
    res = nrow * loc
    per_half = half_res // loc
    lanes = loc * proj
    tiles = proj * seq // 128
    rows = loc * seq
    lo = loc.bit_length() - 1
    sq = seq.bit_length() - 1
    tl = tiles.bit_length() - 1
    br = block_rows(nrow)
    bres = br * loc
    blocks = nrow // br

    grp, row, col = lax.axis_index("grp"), lax.axis_index("row"), lax.axis_index("col")
    other = 1 - col

    def half_of(r):
        return jnp.where(r >= per_half, 1, 0)

    def in_half(r):
        return jnp.where(r >= per_half, r - per_half, r)

    def dev(r, c):
        return (grp, r, c)

    def far_row(k):
        return jnp.where(k >= row, k + 1, k)

    loads = [
        pltpu.make_async_copy(src, dst, isem.at[k])
        for k, (src, dst) in enumerate(
            (
                (x_hbm, x_ref), (wl_hbm, wl_ref), (wr_hbm, wr_ref), (am_hbm, am_ref),
                (rm_hbm, rm_ref), (cot_hbm, cot_ref), (w_hbm, w_ref), (bias_hbm, bias_ref),
            )
        )
    ]
    for load in loads:
        load.start()

    barrier = pltpu.get_barrier_semaphore()

    def greet(k):
        r = far_row(k)
        for c in (col, other):
            pl.semaphore_signal(barrier, inc=1, device_id=dev(r, c), device_id_type=MESH)

    each(nrow - 1, greet)
    pl.semaphore_signal(barrier, inc=1, device_id=dev(row, other), device_id_type=MESH)

    group = iota((seq, 128), 1) >> (proj.bit_length() - 1)

    def pick_group(parts, lane_group):
        out = parts[0]
        for p in range(1, loc):
            out = jnp.where(lane_group == p, parts[p], out)
        return out

    for load in loads[:6]:
        load.wait()

    xf = x_ref[...].astype(F32)
    x = jnp.concatenate([xf[:, r, :] for r in range(loc)], axis=0).astype(BF16)
    pieces = [
        (am_ref[r : r + 1, :] * rm_ref[:, r : r + 1]).astype(F32) for r in range(loc)
    ]
    live = jnp.concatenate([jnp.broadcast_to(p, (seq, seq)) for p in pieces], axis=0)
    diagonal = (iota((rows, seq), 0) & (seq - 1)) == iota((rows, seq), 1)
    live = jnp.sum(jnp.where(diagonal, live, 0.0), axis=1, keepdims=True)
    live = jnp.broadcast_to(live, (rows, 128))
    m_s[...] = jnp.zeros(m_s.shape, F32)
    for r in range(loc):
        m_s[r : r + 1, :seq] = pieces[r]
    factors = jnp.concatenate([wl_ref[...]] * loc + [wr_ref[...]] * loc, axis=0)
    both = mm_t(x, factors)
    left = both[:, :lanes] * live
    right = both[:, lanes:] * live

    def natural(a):
        return pick_group([a[r * seq : (r + 1) * seq] for r in range(loc)], group)

    n_s[0] = natural(left).astype(BF16)
    n_s[1] = natural(right).astype(BF16)
    live_nat = natural(live).astype(BF16)
    lane = iota((rows, 128), 1)
    g = jnp.where(lane < proj, left, live).astype(BF16)
    g_s[:rows] = g
    g_s[rows:] = live_nat

    width = proj * seq
    spread = (iota((128, width), 0) == (iota((128, width), 1) >> sq)).astype(BF16)
    own_seq = (iota((rows, width), 0) & (seq - 1)) == (iota((rows, width), 1) & (seq - 1))
    h = jnp.where(own_seq, mm(right.astype(BF16), spread), 0.0).astype(BF16)
    h = jnp.concatenate([h[:, k * 128 : (k + 1) * 128] for k in range(tiles)], axis=0)
    fr, deep = loc * tiles, tiles * rows
    fi, ki = iota((fr, deep), 0), iota((fr, deep), 1)
    f_row, f_t = fi >> tl, fi & (tiles - 1)
    k_t, k_row = ki >> (lo + sq), (ki >> sq) & (loc - 1)
    pick = ((f_row == k_row) & (f_t == k_t)).astype(BF16)
    f_s[...] = mm(pick, h).astype(BF16)

    cot32 = cot_ref[...].astype(F32)
    if per_half <= UNROLL:
        for q in range(per_half):
            ct_s[q] = jnp.concatenate(
                [cot32[i, q * loc : (q + 1) * loc, :] for i in range(loc)], axis=0
            ).astype(BF16)
    else:
        for i in range(loc):
            c32b[i * half_res : (i + 1) * half_res] = cot32[i]

        @pl.loop(0, per_half)
        def _(q):
            ct_s[q] = jnp.concatenate(
                [c32b[pl.ds(i * half_res + q * loc, loc), :] for i in range(loc)], axis=0
            ).astype(BF16)

    pl.semaphore_wait(barrier, 2 * nrow - 1)

    def copy(src, dst, kind, s_slot, r_slot, to):
        return pltpu.make_async_remote_copy(
            src_ref=src, dst_ref=dst, send_sem=ssem.at[kind, s_slot],
            recv_sem=rsem.at[kind, r_slot], device_id=to, device_id_type=MESH,
        )

    own_half = pl.ds(pl.multiple_of(col * half_res, half_res), half_res)

    def partner(k):
        src, dst = ((g_s, g_r), (cot_ref, cf_r.at[:, own_half, :]))[k]
        return pltpu.make_async_remote_copy(
            src_ref=src, dst_ref=dst, send_sem=psem.at[k], recv_sem=psem.at[2 + k],
            device_id=dev(row, other), device_id_type=MESH,
        )

    def on(pred, f):
        pl.when(pred)(f)

    def send_other(r, act):
        far = half_of(r) == col
        act(copy(m_s, m_r.at[1, row], 5, r, row, dev(r, other)))
        on(far, lambda: act(copy(ct_s.at[in_half(r)], ct_r.at[row], 6, r, row, dev(r, other))))
        on(
            half_of(row) == other,
            lambda: act(copy(f_s, f_r.at[1, in_half(row)], 2, r, row, dev(r, other))),
        )

    def send(k, act):
        r = far_row(k)
        far = half_of(r) == col
        act(copy(m_s, m_r.at[0, row], 4, r, row, dev(r, col)))
        on(far, lambda: act(copy(ct_s.at[in_half(r)], ct_r.at[row], 3, r, row, dev(r, col))))
        act(copy(n_s, n_r.at[row], 0, r, row, dev(r, col)))
        on(
            half_of(row) == col,
            lambda: act(copy(f_s, f_r.at[0, in_half(row)], 1, r, row, dev(r, col))),
        )
        send_other(r, act)

    partner(0).start()
    partner(1).start()
    each(nrow - 1, lambda k: send(k, lambda d: d.start()))
    send_other(row, lambda d: d.start())

    n_r[row] = n_s[...]
    m_r[0, row] = m_s[...]
    cf_r[:, own_half, :] = cot_ref[...]

    @pl.when(half_of(row) == col)
    def _():
        ct_r[row] = ct_s[in_half(row)]
        f_r[0, in_half(row)] = f_s[...]

    loads[6].wait()
    loads[7].wait()
    w32[...] = w_ref[...].astype(F32)
    by_e = [w32[pl.ds(e, proj, stride=proj), :].astype(BF16) for e in range(proj)]
    w_c = jnp.concatenate(by_e, axis=1)

    def turned(k, b):
        return k // loc * loc + (k % loc - b) % loc

    eye = (iota((chan, chan), 0) == iota((chan, chan), 1)).astype(BF16)
    for b in range(loc):
        order = [turned(k, b) for k in range(proj)]
        wt_ref[b] = mm_t(
            eye, jnp.concatenate([w_ref[c * proj : (c + 1) * proj, :] for c in order], axis=0)
        ).astype(BF16)

    def spread_left(gl, part):
        p = mm(gl[:, :proj], w_c).astype(BF16)
        for e in range(proj):
            for i in range(loc):
                p2[part * proj * seq + e * seq : part * proj * seq + (e + 1) * seq,
                   i * chan : (i + 1) * chan] = p[
                    i * seq : (i + 1) * seq, e * chan : (e + 1) * chan
                ]

    def fold(outs, dst):
        lane_group = iota((bres, 128), 1) >> (proj.bit_length() - 1)
        for t in range(proj // loc):
            part = [o[:, t * 128 : (t + 1) * 128] for o in outs]
            for k in range(loc):
                d = pick_group([part[(p - k) % loc] for p in range(loc)], lane_group)
                if k:
                    d = pltpu.roll(d, 128 - k * proj, 1)
                at = (t * loc + k) * bres
                dst[at : at + bres, :] = d

    def block(b):
        if isinstance(b, int):
            return pl.ds(b * bres, bres)
        return pl.ds(pl.multiple_of(b * bres, bres), bres)

    def outer_a(b):
        outs = []
        for i in range(loc):
            order = [turned(k, i) for k in range(proj)]
            outs.append(
                mm_t(cf_r[i, block(b), :], jnp.concatenate([by_e[e] for e in order], axis=0))
            )
        fold(outs, og_a)

    def outer_b(b):
        c32[...] = ct_r[pl.ds(b * br, br)].astype(F32).reshape(bres * loc, chan)
        fold(
            [
                mm(c32[pl.ds(j, bres, stride=loc), :].astype(BF16), wt_ref[j])
                for j in range(loc)
            ],
            og_b,
        )

    def inverse(b):
        total = None
        for k, own in enumerate((live_nat, live_other)):
            m = jnp.concatenate([m_r[k, b * br + r] for r in range(br)], axis=0)
            term = mm(m[:, :seq].astype(BF16), own)
            total = term if total is None else total + term
        inv_ref[block(b), :] = 1.0 / jnp.maximum(total, 1.0)

    def grads(b, dst, og, side, first):
        k = jnp.concatenate(
            [
                (og[pl.ds(r, proj, stride=bres), :] * inv_ref[pl.ds(b * bres + r, 1), :]).astype(BF16)
                for r in range(bres)
            ],
            axis=0,
        )
        a = jnp.concatenate([n_r[b * br + r, side] for r in range(br)], axis=1)
        out = mm(a, k)
        dst[...] = out if first else dst[...] + out

    def arrivals(k, kinds):
        r = far_row(k)
        if 4 in kinds:
            copy(m_s, m_r.at[0, r], 4, r, r, dev(r, col)).wait_recv()
        if 3 in kinds:
            on(
                half_of(row) == col,
                lambda: copy(ct_s.at[0], ct_r.at[r], 3, r, r, dev(r, col)).wait_recv(),
            )
        if 0 in kinds:
            copy(n_s, n_r.at[r], 0, r, r, dev(r, col)).wait_recv()
        if 1 in kinds:
            on(
                half_of(r) == col,
                lambda: copy(f_s, f_r.at[0, in_half(r)], 1, r, r, dev(r, col)).wait_recv(),
            )

    def arrivals_other(r, kinds):
        if 5 in kinds:
            copy(m_s, m_r.at[1, r], 5, r, r, dev(r, other)).wait_recv()
        if 6 in kinds:
            on(
                half_of(row) == other,
                lambda: copy(ct_s.at[0], ct_r.at[r], 6, r, r, dev(r, other)).wait_recv(),
            )
        if 2 in kinds:
            on(
                half_of(r) == col,
                lambda: copy(f_s, f_r.at[1, in_half(r)], 2, r, r, dev(r, other)).wait_recv(),
            )

    spread_left(g, 0)
    partner(0).wait_recv()
    spread_left(g_r[:rows], 1)
    live_other = g_r[rows:]
    partner(1).wait_recv()
    if blocks == 1:
        outer_a(0)
    each(nrow - 1, lambda k: arrivals(k, (3, 4)))
    each(nrow, lambda k: arrivals_other(k, (5, 6)))
    if blocks == 1:
        outer_b(0)
        inverse(0)
    each(nrow - 1, lambda k: arrivals(k, (0,)))
    if blocks == 1:
        grads(0, lg_ref, og_a, 1, True)
        grads(0, rg_ref, og_b, 0, True)
    else:
        lg_ref[...] = jnp.zeros(lg_ref.shape, F32)
        rg_ref[...] = jnp.zeros(rg_ref.shape, F32)

        @pl.loop(0, blocks)
        def _(b):
            outer_a(b)
            outer_b(b)
            inverse(b)
            grads(b, lg_ref, og_a, 1, False)
            grads(b, rg_ref, og_b, 0, False)

    each(nrow - 1, lambda k: arrivals(k, (1,)))
    each(nrow, lambda k: arrivals_other(k, (2,)))
    a32[...] = f_r[...].astype(F32).reshape(2 * half_res * tiles, 128)
    flat = jnp.concatenate(
        [
            a32[pl.ds(k * half_res * tiles + t, half_res, stride=tiles), :]
            for k in range(2)
            for t in range(tiles)
        ],
        axis=1,
    ).astype(BF16)
    mapped = mm(flat, p2[...])
    bias = bias_ref[...]
    own_inv = inv_ref[own_half, :]
    for i in range(loc):
        inv = jnp.broadcast_to(own_inv[:, i * proj : i * proj + 1], (half_res, chan))
        pu_ref[i] = (mapped[:, i * chan : (i + 1) * chan] * inv + bias).astype(BF16)

    partner(0).wait_send()
    partner(1).wait_send()
    each(nrow - 1, lambda k: send(k, lambda d: d.wait_send()))
    send_other(row, lambda d: d.wait_send())


def finish(pu_in, lg_in, rg_in, pu_ref, lg_ref, rg_ref):
    _, loc, proj = lg_ref.shape
    pu_ref[...] = pu_in[...]
    for i in range(loc):
        lg_ref[:, i, :] = lg_in[:, i * proj : (i + 1) * proj]
        rg_ref[:, i, :] = rg_in[:, i * proj : (i + 1) * proj]


def per_device(nrow, x, am, rm, wl, wr, w, bias, cot):
    seq, loc, _ = x.shape
    proj = wl.shape[1]
    half_res, chan = cot.shape[1], cot.shape[2]
    res = nrow * loc
    tiles = proj * seq // 128
    fr = loc * tiles
    rows = loc * seq
    lanes = loc * proj
    per_half = half_res // loc
    bres = block_rows(nrow) * loc
    hbm = pl.BlockSpec(memory_space=pltpu.HBM)
    vm = pl.BlockSpec(memory_space=pltpu.VMEM)
    operands = (x, am.T, rm.reshape(1, loc), wl.T, wr.T, w, bias.reshape(1, chan), cot)
    held = [pltpu.with_memory_space_constraint(a, pltpu.HBM) for a in operands]
    pu, lg, rg = pl.pallas_call(
        functools.partial(kernel, nrow),
        out_shape=(
            jax.ShapeDtypeStruct(cot.shape, BF16),
            jax.ShapeDtypeStruct((seq, lanes), F32),
            jax.ShapeDtypeStruct((seq, lanes), F32),
        ),
        in_specs=[hbm] * 8,
        out_specs=(vm, vm, vm),
        scratch_shapes=[pltpu.VMEM(a.shape, a.dtype) for a in operands]
        + [
            pltpu.VMEM((rows + seq, 128), BF16),
            pltpu.VMEM((rows + seq, 128), BF16),
            pltpu.VMEM((2, seq, lanes), BF16),
            pltpu.VMEM((nrow, 2, seq, lanes), BF16),
            pltpu.VMEM((fr, 128), BF16),
            pltpu.VMEM((2, per_half, fr, 128), BF16),
            pltpu.VMEM((per_half, loc * loc, chan), BF16),
            pltpu.VMEM((nrow, loc * loc, chan), BF16),
            pltpu.VMEM((loc, res, chan), BF16),
            pltpu.VMEM((loc, 128), F32),
            pltpu.VMEM((2, nrow, loc, 128), F32),
            pltpu.VMEM((proj * proj, chan), F32),
            pltpu.VMEM((2 * half_res * tiles, 128), F32),
            pltpu.VMEM((bres * loc, chan), F32),
            pltpu.VMEM((loc * half_res, chan), F32),
            pltpu.VMEM((res, lanes), F32),
            pltpu.VMEM((proj * bres, lanes), F32),
            pltpu.VMEM((proj * bres, lanes), F32),
            pltpu.VMEM((loc, chan, proj * proj), BF16),
            pltpu.VMEM((2 * proj * seq, loc * chan), BF16),
            pltpu.SemaphoreType.DMA((7, nrow)),
            pltpu.SemaphoreType.DMA((7, nrow)),
            pltpu.SemaphoreType.DMA((4,)),
            pltpu.SemaphoreType.DMA((8,)),
        ],
        compiler_params=pltpu.CompilerParams(
            collective_id=0, has_side_effects=True, vmem_limit_bytes=GRANT
        ),
    )(*held)
    grads = jax.ShapeDtypeStruct((seq, loc, proj), F32)
    return pl.pallas_call(
        finish,
        out_shape=(jax.ShapeDtypeStruct(cot.shape, BF16), grads, grads),
        in_specs=[vm] * 3,
        out_specs=(vm, vm, vm),
        compiler_params=pltpu.CompilerParams(vmem_limit_bytes=GRANT),
    )(pu, lg, rg)


def solution(mesh):
    placed = (
        P(("grp", "col"), "row", None),
        P(("grp", "col"), "row"),
        P(("grp", "row")),
        P(),
        P(),
        P(),
        P(),
        P(("grp", "row"), "col", None),
    )
    return jax.shard_map(
        functools.partial(per_device, mesh.shape["row"]),
        mesh=mesh,
        in_specs=placed,
        out_specs=(
            P(("grp", "row"), "col", None),
            P(("grp", "col"), "row", None),
            P(("grp", "col"), "row", None),
        ),
        check_vma=False,
    )
```

```python
import functools

import jax
import jax.numpy as jnp
from jax import lax
from jax.experimental import pallas as pl
from jax.experimental.pallas import tpu as pltpu
from jax.sharding import PartitionSpec as P

F32 = jnp.float32
BF16 = jnp.bfloat16
MESH = pl.DeviceIdType.MESH
UNROLL = 8
GRANT = 40 << 20
PAD = 4


def iota(shape, axis):
    return lax.broadcasted_iota(jnp.int32, shape, axis)


def mm(a, b):
    return lax.dot_general(a, b, (((1,), (0,)), ((), ())), preferred_element_type=F32)


def mm_t(a, b):
    return lax.dot_general(a, b, (((1,), (1,)), ((), ())), preferred_element_type=F32)


def each(n, f):
    if n <= UNROLL:
        for k in range(n):
            f(k)
    else:

        @pl.loop(0, n)
        def _(k):
            f(k)


def block_rows(nrow):
    n = min(nrow, 8)
    while nrow % n:
        n -= 1
    return n


def kernel(
    nrow,
    x_hbm, am_hbm, rm_hbm, wl_hbm, wr_hbm, w_hbm, bias_hbm, cot_hbm,
    pu_ref, lg_ref, rg_ref,
    x_ref, am_ref, rm_ref, wl_ref, wr_ref, w_ref, bias_ref, cot_ref,
    g_s, g_r, n_s, n_r, f_s, f_r, ct_s, ct_r, cf_r, m_s, m_r,
    w32, a32, c32, c32b, inv_ref, og_a, og_b, k_a, k_b, wt_ref, p2,
    ssem, rsem, isem,
):
    seq, loc, feat = x_ref.shape
    proj = wl_ref.shape[0]
    half_res, chan = cot_ref.shape[1], cot_ref.shape[2]
    res = nrow * loc
    per_half = half_res // loc
    lanes = loc * proj
    tiles = proj * seq // 128
    rows = loc * seq
    lo = loc.bit_length() - 1
    sq = seq.bit_length() - 1
    tl = tiles.bit_length() - 1
    br = block_rows(nrow)
    bres = br * loc
    blocks = nrow // br

    grp, row, col = lax.axis_index("grp"), lax.axis_index("row"), lax.axis_index("col")
    other = 1 - col

    def half_of(r):
        return jnp.where(r >= per_half, 1, 0)

    def in_half(r):
        return jnp.where(r >= per_half, r - per_half, r)

    def dev(r, c):
        return (grp, r, c)

    def far_row(k):
        if nrow % 2:
            return jnp.where(k >= row, k + 1, k)
        p = lax.rem(row, 2)
        k = jnp.where(k >= row - p, k + 1, k)
        return k + p * (1 - 2 * lax.rem(k, 2))

    loads = [
        pltpu.make_async_copy(src, dst, isem.at[k])
        for k, (src, dst) in enumerate(
            (
                (x_hbm, x_ref), (wl_hbm, wl_ref), (wr_hbm, wr_ref), (am_hbm, am_ref),
                (rm_hbm, rm_ref), (cot_hbm, cot_ref), (w_hbm, w_ref), (bias_hbm, bias_ref),
            )
        )
    ]
    for load in loads:
        load.start()

    barrier = pltpu.get_barrier_semaphore()

    def greet(k):
        r = far_row(k)
        for c in (col, other):
            pl.semaphore_signal(barrier, inc=1, device_id=dev(r, c), device_id_type=MESH)

    each(nrow - 1, greet)
    pl.semaphore_signal(barrier, inc=1, device_id=dev(row, other), device_id_type=MESH)

    group = iota((seq, 128), 1) >> (proj.bit_length() - 1)

    def pick_group(parts, lane_group):
        out = parts[0]
        for p in range(1, loc):
            out = jnp.where(lane_group == p, parts[p], out)
        return out

    for load in loads[:6]:
        load.wait()

    xf = x_ref[...].astype(F32)
    x = jnp.concatenate([xf[:, r, :] for r in range(loc)], axis=0).astype(BF16)
    pieces = [
        (am_ref[r : r + 1, :] * rm_ref[:, r : r + 1]).astype(F32) for r in range(loc)
    ]
    live = jnp.concatenate([jnp.broadcast_to(p, (seq, seq)) for p in pieces], axis=0)
    diagonal = (iota((rows, seq), 0) & (seq - 1)) == iota((rows, seq), 1)
    live = jnp.sum(jnp.where(diagonal, live, 0.0), axis=1, keepdims=True)
    live = jnp.broadcast_to(live, (rows, 128))
    lane = iota((rows, 128), 1)
    m_s[...] = jnp.sum(jnp.where(lane == iota((rows, 128), 0), live, 0.0), axis=0, keepdims=True)
    factors = jnp.concatenate([wl_ref[...]] * loc + [wr_ref[...]] * loc, axis=0)
    both = mm_t(x, factors)
    left = both[:, :lanes] * live
    right = both[:, lanes:] * live

    def natural(a):
        return pick_group([a[r * seq : (r + 1) * seq] for r in range(loc)], group)

    n_s[0] = natural(left).astype(BF16)
    n_s[1] = natural(right).astype(BF16)
    live_nat = natural(live).astype(BF16)
    g = jnp.where(lane < proj, left, live).astype(BF16)
    g_s[:rows] = g
    g_s[rows:] = live_nat

    width = proj * seq
    spread = (iota((128, width), 0) == (iota((128, width), 1) >> sq)).astype(BF16)
    own_seq = (iota((rows, width), 0) & (seq - 1)) == (iota((rows, width), 1) & (seq - 1))
    h = jnp.where(own_seq, mm(right.astype(BF16), spread), 0.0).astype(BF16)
    h = jnp.concatenate([h[:, k * 128 : (k + 1) * 128] for k in range(tiles)], axis=0)
    fr, deep = loc * tiles, tiles * rows
    fi, ki = iota((fr, deep), 0), iota((fr, deep), 1)
    f_row, f_t = fi >> tl, fi & (tiles - 1)
    k_t, k_row = ki >> (lo + sq), (ki >> sq) & (loc - 1)
    pick = ((f_row == k_row) & (f_t == k_t)).astype(BF16)
    f_s[...] = mm(pick, h).astype(BF16)

    cot32 = cot_ref[...].astype(F32)
    if per_half <= UNROLL:
        for q in range(per_half):
            ct_s[q] = jnp.concatenate(
                [cot32[i, q * loc : (q + 1) * loc, :] for i in range(loc)], axis=0
            ).astype(BF16)
    else:
        for i in range(loc):
            c32b[i * half_res : (i + 1) * half_res] = cot32[i]

        @pl.loop(0, per_half)
        def _(q):
            ct_s[q] = jnp.concatenate(
                [c32b[pl.ds(i * half_res + q * loc, loc), :] for i in range(loc)], axis=0
            ).astype(BF16)

    pl.semaphore_wait(barrier, 2 * nrow - 1)

    def copy(src, dst, kind, to):
        return pltpu.make_async_remote_copy(
            src_ref=src, dst_ref=dst, send_sem=ssem.at[kind], recv_sem=rsem.at[kind],
            device_id=to, device_id_type=MESH,
        )

    def drain(ref, count, sem):
        view = ref.at[pl.ds(0, count)]
        pltpu.make_async_copy(view, view, sem).wait()

    own_half = pl.ds(pl.multiple_of(col * half_res, half_res), half_res)
    inside = half_of(row) == col
    mine = in_half(row)

    def partner(k):
        src, dst = ((g_s, g_r), (cot_ref, cf_r.at[:, own_half, :]))[k]
        return copy(src, dst, k, dev(row, other))

    def on(pred, f):
        pl.when(pred)(f)

    def send_other(r):
        copy(m_s, m_r.at[nrow + row], 2, dev(r, other)).start()
        on(
            half_of(r) == col,
            lambda: copy(ct_s.at[in_half(r)], ct_r.at[row], 3, dev(r, other)).start(),
        )
        on(
            half_of(row) == other,
            lambda: copy(f_s, f_r.at[per_half + mine], 5, dev(r, other)).start(),
        )

    def send(k):
        r = far_row(k)
        copy(m_s, m_r.at[row], 2, dev(r, col)).start()
        on(
            half_of(r) == col,
            lambda: copy(ct_s.at[in_half(r)], ct_r.at[row], 3, dev(r, col)).start(),
        )
        copy(n_s, n_r.at[row], 4, dev(r, col)).start()
        on(inside, lambda: copy(f_s, f_r.at[mine], 5, dev(r, col)).start())
        send_other(r)

    partner(0).start()
    partner(1).start()
    each(nrow - 1, send)
    send_other(row)

    def drain_some(ref, kind, sem, less):
        on(less, lambda: drain(ref, nrow - 1, sem.at[kind]))
        on(jnp.logical_not(less), lambda: drain(ref, nrow, sem.at[kind]))

    n_r[row] = n_s[...]
    m_r[row] = m_s[...]
    cf_r[:, own_half, :] = cot_ref[...]

    @pl.when(inside)
    def _():
        ct_r[row] = ct_s[mine]
        f_r[mine] = f_s[...]

    loads[6].wait()
    loads[7].wait()
    for c in range(proj):
        w32[c * (proj + PAD) : c * (proj + PAD) + proj, :] = w_ref[
            c * proj : (c + 1) * proj, :
        ].astype(F32)
    by_e = [w32[pl.ds(e, proj, stride=proj + PAD), :].astype(BF16) for e in range(proj)]
    w_c = jnp.concatenate(by_e, axis=1)

    def turned(k, b):
        return k // loc * loc + (k % loc - b) % loc

    eye = (iota((chan, chan), 0) == iota((chan, chan), 1)).astype(BF16)
    for b in range(loc):
        order = [turned(k, b) for k in range(proj)]
        wt_ref[b] = mm_t(
            eye, jnp.concatenate([w_ref[c * proj : (c + 1) * proj, :] for c in order], axis=0)
        ).astype(BF16)

    def spread_left(gl, part):
        p = mm(gl[:, :proj], w_c).astype(BF16)
        for e in range(proj):
            for i in range(loc):
                p2[part * proj * seq + e * seq : part * proj * seq + (e + 1) * seq,
                   i * chan : (i + 1) * chan] = p[
                    i * seq : (i + 1) * seq, e * chan : (e + 1) * chan
                ]

    def fold(outs, dst):
        lane_group = iota((bres, 128), 1) >> (proj.bit_length() - 1)
        for t in range(proj // loc):
            part = [o[:, t * 128 : (t + 1) * 128] for o in outs]
            for k in range(loc):
                d = pick_group([part[(p - k) % loc] for p in range(loc)], lane_group)
                if k:
                    d = pltpu.roll(d, 128 - k * proj, 1)
                at = (t * loc + k) * (bres + PAD)
                dst[at : at + bres, :] = d

    def block(b):
        if isinstance(b, int):
            return pl.ds(b * bres, bres)
        return pl.ds(pl.multiple_of(b * bres, bres), bres)

    def outer_a(b):
        outs = []
        for i in range(loc):
            order = [turned(k, i) for k in range(proj)]
            outs.append(
                mm_t(cf_r[i, block(b), :], jnp.concatenate([by_e[e] for e in order], axis=0))
            )
        fold(outs, og_a)

    def outer_b(b):
        c32[...] = ct_r[pl.ds(b * br, br)].astype(F32).reshape(bres * loc, chan)
        fold(
            [
                mm(c32[pl.ds(j, bres, stride=loc), :].astype(BF16), wt_ref[j])
                for j in range(loc)
            ],
            og_b,
        )

    def inverse(b):
        spot = (iota((bres, br), 0) >> lo == iota((bres, br), 1)).astype(BF16)
        own_lane = (iota((bres, 128), 0) & (loc - 1)) == (iota((bres, 128), 1) >> sq)
        total = None
        for k, own in enumerate((live_nat, live_other)):
            m = m_r[pl.ds(k * nrow + b * br, br)].reshape(br, 128).astype(BF16)
            m = jnp.where(own_lane, mm(spot, m), 0.0).astype(BF16)
            term = mm(m, jnp.concatenate([own] * (128 // seq), axis=0))
            total = term if total is None else total + term
        inv_ref[block(b), :] = 1.0 / jnp.maximum(total, 1.0)

    def operator(b, og, dst):
        for r in range(bres):
            dst[r * proj : (r + 1) * proj, :] = (
                og[pl.ds(r, proj, stride=bres + PAD), :] * inv_ref[pl.ds(b * bres + r, 1), :]
            ).astype(BF16)

    def grads(b, dst, k_ref, side, first):
        a = jnp.concatenate([n_r[b * br + r, side] for r in range(br)], axis=1)
        out = mm(a, k_ref[...])
        dst[...] = out if first else dst[...] + out

    spread_left(g, 0)
    partner(0).wait_recv()
    spread_left(g_r[:rows], 1)
    live_other = g_r[rows:]
    partner(1).wait_recv()
    if blocks == 1:
        outer_a(0)
    drain(m_r, 2 * nrow - 1, rsem.at[2])
    drain_some(ct_r, 3, rsem, inside)
    if blocks == 1:
        inverse(0)
        operator(0, og_a, k_a)
        outer_b(0)
        operator(0, og_b, k_b)
    drain(n_r, nrow - 1, rsem.at[4])
    if blocks == 1:
        grads(0, lg_ref, k_a, 1, True)
        grads(0, rg_ref, k_b, 0, True)
    else:
        lg_ref[...] = jnp.zeros(lg_ref.shape, F32)
        rg_ref[...] = jnp.zeros(rg_ref.shape, F32)

        @pl.loop(0, blocks)
        def _(b):
            outer_a(b)
            outer_b(b)
            inverse(b)
            operator(b, og_a, k_a)
            operator(b, og_b, k_b)
            grads(b, lg_ref, k_a, 1, False)
            grads(b, rg_ref, k_b, 0, False)

    drain_some(f_r, 5, rsem, inside)
    a32[...] = f_r[...].astype(F32).reshape(2 * half_res * tiles, 128)
    flat = jnp.concatenate(
        [
            a32[pl.ds(k * half_res * tiles + t, half_res, stride=tiles), :]
            for k in range(2)
            for t in range(tiles)
        ],
        axis=1,
    ).astype(BF16)
    mapped = mm(flat, p2[...])
    bias = bias_ref[...]
    own_inv = inv_ref[own_half, :]
    for i in range(loc):
        inv = jnp.broadcast_to(own_inv[:, i * proj : i * proj + 1], (half_res, chan))
        pu_ref[i] = (mapped[:, i * chan : (i + 1) * chan] * inv + bias).astype(BF16)

    partner(0).wait_send()
    partner(1).wait_send()
    drain(m_r, 2 * nrow - 1, ssem.at[2])
    drain_some(ct_r, 3, ssem, inside)
    drain(n_r, nrow - 1, ssem.at[4])
    drain_some(f_r, 5, ssem, inside)


def finish(pu_in, lg_in, rg_in, pu_ref, lg_ref, rg_ref):
    _, loc, proj = lg_ref.shape
    pu_ref[...] = pu_in[...]
    for i in range(loc):
        lg_ref[:, i, :] = lg_in[:, i * proj : (i + 1) * proj]
        rg_ref[:, i, :] = rg_in[:, i * proj : (i + 1) * proj]


def per_device(nrow, x, am, rm, wl, wr, w, bias, cot):
    seq, loc, _ = x.shape
    proj = wl.shape[1]
    half_res, chan = cot.shape[1], cot.shape[2]
    res = nrow * loc
    tiles = proj * seq // 128
    fr = loc * tiles
    rows = loc * seq
    lanes = loc * proj
    per_half = half_res // loc
    bres = block_rows(nrow) * loc
    hbm = pl.BlockSpec(memory_space=pltpu.HBM)
    vm = pl.BlockSpec(memory_space=pltpu.VMEM)
    operands = (x, am.T, rm.reshape(1, loc), wl.T, wr.T, w, bias.reshape(1, chan), cot)
    held = [pltpu.with_memory_space_constraint(a, pltpu.HBM) for a in operands]
    pu, lg, rg = pl.pallas_call(
        functools.partial(kernel, nrow),
        out_shape=(
            jax.ShapeDtypeStruct(cot.shape, BF16),
            jax.ShapeDtypeStruct((seq, lanes), F32),
            jax.ShapeDtypeStruct((seq, lanes), F32),
        ),
        in_specs=[hbm] * 8,
        out_specs=(vm, vm, vm),
        scratch_shapes=[pltpu.VMEM(a.shape, a.dtype) for a in operands]
        + [
            pltpu.VMEM((rows + seq, 128), BF16),
            pltpu.VMEM((rows + seq, 128), BF16),
            pltpu.VMEM((2, seq, lanes), BF16),
            pltpu.VMEM((nrow, 2, seq, lanes), BF16),
            pltpu.VMEM((fr, 128), BF16),
            pltpu.VMEM((nrow, fr, 128), BF16),
            pltpu.VMEM((per_half, loc * loc, chan), BF16),
            pltpu.VMEM((nrow, loc * loc, chan), BF16),
            pltpu.VMEM((loc, res, chan), BF16),
            pltpu.VMEM((1, 128), F32),
            pltpu.VMEM((2 * nrow, 1, 128), F32),
            pltpu.VMEM((proj * (proj + PAD), chan), F32),
            pltpu.VMEM((2 * half_res * tiles, 128), F32),
            pltpu.VMEM((bres * loc, chan), F32),
            pltpu.VMEM((loc * half_res, chan), F32),
            pltpu.VMEM((res, lanes), F32),
            pltpu.VMEM((proj * (bres + PAD), lanes), F32),
            pltpu.VMEM((proj * (bres + PAD), lanes), F32),
            pltpu.VMEM((bres * proj, lanes), BF16),
            pltpu.VMEM((bres * proj, lanes), BF16),
            pltpu.VMEM((loc, chan, proj * proj), BF16),
            pltpu.VMEM((2 * proj * seq, loc * chan), BF16),
            pltpu.SemaphoreType.DMA((6,)),
            pltpu.SemaphoreType.DMA((6,)),
            pltpu.SemaphoreType.DMA((8,)),
        ],
        compiler_params=pltpu.CompilerParams(
            collective_id=0, has_side_effects=True, vmem_limit_bytes=GRANT
        ),
    )(*held)
    grads = jax.ShapeDtypeStruct((seq, loc, proj), F32)
    return pl.pallas_call(
        finish,
        out_shape=(jax.ShapeDtypeStruct(cot.shape, BF16), grads, grads),
        in_specs=[vm] * 3,
        out_specs=(vm, vm, vm),
        compiler_params=pltpu.CompilerParams(vmem_limit_bytes=GRANT),
    )(pu, lg, rg)


def solution(mesh):
    placed = (
        P(("grp", "col"), "row", None),
        P(("grp", "col"), "row"),
        P(("grp", "row")),
        P(),
        P(),
        P(),
        P(),
        P(("grp", "row"), "col", None),
    )
    return jax.shard_map(
        functools.partial(per_device, mesh.shape["row"]),
        mesh=mesh,
        in_specs=placed,
        out_specs=(
            P(("grp", "row"), "col", None),
            P(("grp", "col"), "row", None),
            P(("grp", "col"), "row", None),
        ),
        check_vma=False,
    )
```

```python
import functools

import jax
import jax.numpy as jnp
from jax import lax
from jax.experimental import pallas as pl
from jax.experimental.pallas import tpu as pltpu
from jax.sharding import PartitionSpec as P

F32 = jnp.float32
BF16 = jnp.bfloat16
MESH = pl.DeviceIdType.MESH
UNROLL = 8
GRANT = 40 << 20
PAD = 4


def iota(shape, axis):
    return lax.broadcasted_iota(jnp.int32, shape, axis)


def mm(a, b):
    return lax.dot_general(a, b, (((1,), (0,)), ((), ())), preferred_element_type=F32)


def mm_t(a, b):
    return lax.dot_general(a, b, (((1,), (1,)), ((), ())), preferred_element_type=F32)


def each(n, f):
    if n <= UNROLL:
        for k in range(n):
            f(k)
    else:

        @pl.loop(0, n)
        def _(k):
            f(k)


def block_rows(nrow):
    n = min(nrow, 8)
    while nrow % n:
        n -= 1
    return n


def kernel(
    nrow,
    x_hbm, am_hbm, rm_hbm, wl_hbm, wr_hbm, w_hbm, bias_hbm, cot_hbm,
    pu_ref, lg_ref, rg_ref,
    x_ref, am_ref, rm_ref, wl_ref, wr_ref, w_ref, bias_ref, cot_ref,
    g_s, g_r, n_s, n_r, f_s, f_r, ct_s, ct_r, cf_r, m_s, m_r,
    w32, a32, c32, c32b, inv_ref, og_a, og_b, k_a, k_b, wt_ref, p2,
    ssem, rsem, isem,
):
    seq, loc, feat = x_ref.shape
    proj = wl_ref.shape[0]
    half_res, chan = cot_ref.shape[1], cot_ref.shape[2]
    res = nrow * loc
    per_half = half_res // loc
    lanes = loc * proj
    tiles = proj * seq // 128
    rows = loc * seq
    lo = loc.bit_length() - 1
    sq = seq.bit_length() - 1
    tl = tiles.bit_length() - 1
    br = block_rows(nrow)
    bres = br * loc
    blocks = nrow // br

    grp, row, col = lax.axis_index("grp"), lax.axis_index("row"), lax.axis_index("col")
    other = 1 - col

    def half_of(r):
        return jnp.where(r >= per_half, 1, 0)

    def in_half(r):
        return jnp.where(r >= per_half, r - per_half, r)

    def dev(r, c):
        return (grp, r, c)

    def far_row(k):
        return jnp.where(k >= row, k + 1, k)

    loads = [
        pltpu.make_async_copy(src, dst, isem.at[k])
        for k, (src, dst) in enumerate(
            (
                (x_hbm, x_ref), (wl_hbm, wl_ref), (wr_hbm, wr_ref), (am_hbm, am_ref),
                (rm_hbm, rm_ref), (cot_hbm, cot_ref), (w_hbm, w_ref), (bias_hbm, bias_ref),
            )
        )
    ]
    for load in loads:
        load.start()

    barrier = pltpu.get_barrier_semaphore()

    def greet(k):
        r = far_row(k)
        for c in (col, other):
            pl.semaphore_signal(barrier, inc=1, device_id=dev(r, c), device_id_type=MESH)

    each(nrow - 1, greet)
    pl.semaphore_signal(barrier, inc=1, device_id=dev(row, other), device_id_type=MESH)

    group = iota((seq, 128), 1) >> (proj.bit_length() - 1)

    def pick_group(parts, lane_group):
        out = parts[0]
        for p in range(1, loc):
            out = jnp.where(lane_group == p, parts[p], out)
        return out

    for load in loads[:6]:
        load.wait()

    xf = x_ref[...].astype(F32)
    x = jnp.concatenate([xf[:, r, :] for r in range(loc)], axis=0).astype(BF16)
    pieces = [
        (am_ref[r : r + 1, :] * rm_ref[:, r : r + 1]).astype(F32) for r in range(loc)
    ]
    live = jnp.concatenate([jnp.broadcast_to(p, (seq, seq)) for p in pieces], axis=0)
    diagonal = (iota((rows, seq), 0) & (seq - 1)) == iota((rows, seq), 1)
    live = jnp.sum(jnp.where(diagonal, live, 0.0), axis=1, keepdims=True)
    live = jnp.broadcast_to(live, (rows, 128))
    lane = iota((rows, 128), 1)
    m_s[...] = jnp.sum(jnp.where(lane == iota((rows, 128), 0), live, 0.0), axis=0, keepdims=True)
    factors = jnp.concatenate([wl_ref[...]] * loc + [wr_ref[...]] * loc, axis=0)
    both = mm_t(x, factors)
    left = both[:, :lanes] * live
    right = both[:, lanes:] * live

    def natural(a):
        return pick_group([a[r * seq : (r + 1) * seq] for r in range(loc)], group)

    n_s[0] = natural(left).astype(BF16)
    n_s[1] = natural(right).astype(BF16)
    live_nat = natural(live).astype(BF16)
    g = jnp.where(lane < proj, left, live).astype(BF16)
    g_s[:rows] = g
    g_s[rows:] = live_nat

    width = proj * seq
    spread = (iota((128, width), 0) == (iota((128, width), 1) >> sq)).astype(BF16)
    own_seq = (iota((rows, width), 0) & (seq - 1)) == (iota((rows, width), 1) & (seq - 1))
    h = jnp.where(own_seq, mm(right.astype(BF16), spread), 0.0).astype(BF16)
    h = jnp.concatenate([h[:, k * 128 : (k + 1) * 128] for k in range(tiles)], axis=0)
    fr, deep = loc * tiles, tiles * rows
    fi, ki = iota((fr, deep), 0), iota((fr, deep), 1)
    f_row, f_t = fi >> tl, fi & (tiles - 1)
    k_t, k_row = ki >> (lo + sq), (ki >> sq) & (loc - 1)
    pick = ((f_row == k_row) & (f_t == k_t)).astype(BF16)
    f_s[...] = mm(pick, h).astype(BF16)

    cot32 = cot_ref[...].astype(F32)
    if per_half <= UNROLL:
        for q in range(per_half):
            ct_s[q] = jnp.concatenate(
                [cot32[i, q * loc : (q + 1) * loc, :] for i in range(loc)], axis=0
            ).astype(BF16)
    else:
        for i in range(loc):
            c32b[i * half_res : (i + 1) * half_res] = cot32[i]

        @pl.loop(0, per_half)
        def _(q):
            ct_s[q] = jnp.concatenate(
                [c32b[pl.ds(i * half_res + q * loc, loc), :] for i in range(loc)], axis=0
            ).astype(BF16)

    pl.semaphore_wait(barrier, 2 * nrow - 1)

    def copy(src, dst, kind, to):
        return pltpu.make_async_remote_copy(
            src_ref=src, dst_ref=dst, send_sem=ssem.at[kind], recv_sem=rsem.at[kind],
            device_id=to, device_id_type=MESH,
        )

    def drain(ref, count, sem):
        view = ref.at[pl.ds(0, count)]
        pltpu.make_async_copy(view, view, sem).wait()

    own_half = pl.ds(pl.multiple_of(col * half_res, half_res), half_res)
    inside = half_of(row) == col
    mine = in_half(row)

    def partner(k):
        src, dst = ((g_s, g_r), (cot_ref, cf_r.at[:, own_half, :]))[k]
        return copy(src, dst, k, dev(row, other))

    def on(pred, f):
        pl.when(pred)(f)

    def send_other(r):
        copy(m_s, m_r.at[nrow + row], 2, dev(r, other)).start()
        on(
            half_of(r) == col,
            lambda: copy(ct_s.at[in_half(r)], ct_r.at[row], 3, dev(r, other)).start(),
        )
        on(
            half_of(row) == other,
            lambda: copy(f_s, f_r.at[per_half + mine], 5, dev(r, other)).start(),
        )

    def send(k):
        r = far_row(k)
        copy(m_s, m_r.at[row], 2, dev(r, col)).start()
        on(
            half_of(r) == col,
            lambda: copy(ct_s.at[in_half(r)], ct_r.at[row], 3, dev(r, col)).start(),
        )
        copy(n_s, n_r.at[row], 4, dev(r, col)).start()
        on(inside, lambda: copy(f_s, f_r.at[mine], 5, dev(r, col)).start())
        send_other(r)

    partner(0).start()
    partner(1).start()
    each(nrow - 1, send)
    send_other(row)

    def drain_some(ref, kind, sem, less):
        on(less, lambda: drain(ref, nrow - 1, sem.at[kind]))
        on(jnp.logical_not(less), lambda: drain(ref, nrow, sem.at[kind]))

    n_r[row] = n_s[...]
    m_r[row] = m_s[...]
    cf_r[:, own_half, :] = cot_ref[...]

    @pl.when(inside)
    def _():
        ct_r[row] = ct_s[mine]
        f_r[mine] = f_s[...]

    loads[6].wait()
    loads[7].wait()
    for c in range(proj):
        w32[c * (proj + PAD) : c * (proj + PAD) + proj, :] = w_ref[
            c * proj : (c + 1) * proj, :
        ].astype(F32)
    by_e = [w32[pl.ds(e, proj, stride=proj + PAD), :].astype(BF16) for e in range(proj)]
    w_c = jnp.concatenate(by_e, axis=1)

    def turned(k, b):
        return k // loc * loc + (k % loc - b) % loc

    eye = (iota((chan, chan), 0) == iota((chan, chan), 1)).astype(BF16)
    for b in range(loc):
        order = [turned(k, b) for k in range(proj)]
        wt_ref[b] = mm_t(
            eye, jnp.concatenate([w_ref[c * proj : (c + 1) * proj, :] for c in order], axis=0)
        ).astype(BF16)

    def spread_left(gl, part):
        p = mm(gl[:, :proj], w_c).astype(BF16)
        for e in range(proj):
            for i in range(loc):
                p2[part * proj * seq + e * seq : part * proj * seq + (e + 1) * seq,
                   i * chan : (i + 1) * chan] = p[
                    i * seq : (i + 1) * seq, e * chan : (e + 1) * chan
                ]

    def fold(outs, dst):
        lane_group = iota((bres, 128), 1) >> (proj.bit_length() - 1)
        for t in range(proj // loc):
            part = [o[:, t * 128 : (t + 1) * 128] for o in outs]
            for k in range(loc):
                d = pick_group([part[(p - k) % loc] for p in range(loc)], lane_group)
                if k:
                    d = pltpu.roll(d, 128 - k * proj, 1)
                at = (t * loc + k) * (bres + PAD)
                dst[at : at + bres, :] = d

    def block(b):
        if isinstance(b, int):
            return pl.ds(b * bres, bres)
        return pl.ds(pl.multiple_of(b * bres, bres), bres)

    def outer_a(b):
        outs = []
        for i in range(loc):
            order = [turned(k, i) for k in range(proj)]
            outs.append(
                mm_t(cf_r[i, block(b), :], jnp.concatenate([by_e[e] for e in order], axis=0))
            )
        fold(outs, og_a)

    def outer_b(b):
        c32[...] = ct_r[pl.ds(b * br, br)].astype(F32).reshape(bres * loc, chan)
        fold(
            [
                mm(c32[pl.ds(j, bres, stride=loc), :].astype(BF16), wt_ref[j])
                for j in range(loc)
            ],
            og_b,
        )

    def inverse(b):
        spot = (iota((bres, br), 0) >> lo == iota((bres, br), 1)).astype(BF16)
        own_lane = (iota((bres, 128), 0) & (loc - 1)) == (iota((bres, 128), 1) >> sq)
        total = None
        for k, own in enumerate((live_nat, live_other)):
            m = m_r[pl.ds(k * nrow + b * br, br)].reshape(br, 128).astype(BF16)
            m = jnp.where(own_lane, mm(spot, m), 0.0).astype(BF16)
            term = mm(m, jnp.concatenate([own] * (128 // seq), axis=0))
            total = term if total is None else total + term
        inv_ref[block(b), :] = 1.0 / jnp.maximum(total, 1.0)

    def operator(b, og, dst):
        for r in range(bres):
            dst[r * proj : (r + 1) * proj, :] = (
                og[pl.ds(r, proj, stride=bres + PAD), :] * inv_ref[pl.ds(b * bres + r, 1), :]
            ).astype(BF16)

    def grads(b, dst, k_ref, side, first):
        a = jnp.concatenate([n_r[b * br + r, side] for r in range(br)], axis=1)
        out = mm(a, k_ref[...])
        for i in range(loc):
            at = pl.ds(i, seq, stride=loc)
            part = out[:, i * proj : (i + 1) * proj]
            dst[at, :] = part if first else dst[at, :] + part

    spread_left(g, 0)
    partner(0).wait_recv()
    spread_left(g_r[:rows], 1)
    live_other = g_r[rows:]
    partner(1).wait_recv()
    if blocks == 1:
        outer_a(0)
    drain(m_r, 2 * nrow - 1, rsem.at[2])
    drain_some(ct_r, 3, rsem, inside)
    if blocks == 1:
        inverse(0)
        operator(0, og_a, k_a)
        outer_b(0)
        operator(0, og_b, k_b)
    drain(n_r, nrow - 1, rsem.at[4])
    if blocks == 1:
        grads(0, lg_ref, k_a, 1, True)
        grads(0, rg_ref, k_b, 0, True)
    else:
        lg_ref[...] = jnp.zeros(lg_ref.shape, F32)
        rg_ref[...] = jnp.zeros(rg_ref.shape, F32)

        @pl.loop(0, blocks)
        def _(b):
            outer_a(b)
            outer_b(b)
            inverse(b)
            operator(b, og_a, k_a)
            operator(b, og_b, k_b)
            grads(b, lg_ref, k_a, 1, False)
            grads(b, rg_ref, k_b, 0, False)

    drain_some(f_r, 5, rsem, inside)
    a32[...] = f_r[...].astype(F32).reshape(2 * half_res * tiles, 128)
    flat = jnp.concatenate(
        [
            a32[pl.ds(k * half_res * tiles + t, half_res, stride=tiles), :]
            for k in range(2)
            for t in range(tiles)
        ],
        axis=1,
    ).astype(BF16)
    mapped = mm(flat, p2[...])
    bias = bias_ref[...]
    own_inv = inv_ref[own_half, :]
    for i in range(loc):
        inv = jnp.broadcast_to(own_inv[:, i * proj : i * proj + 1], (half_res, chan))
        pu_ref[i] = (mapped[:, i * chan : (i + 1) * chan] * inv + bias).astype(BF16)

    partner(0).wait_send()
    partner(1).wait_send()
    drain(m_r, 2 * nrow - 1, ssem.at[2])
    drain_some(ct_r, 3, ssem, inside)
    drain(n_r, nrow - 1, ssem.at[4])
    drain_some(f_r, 5, ssem, inside)


def finish(pu_in, lg_in, rg_in, pu_ref, lg_ref, rg_ref):
    pu_ref[...] = pu_in[...]
    lg_ref[...] = lg_in[...]
    rg_ref[...] = rg_in[...]


def per_device(nrow, x, am, rm, wl, wr, w, bias, cot):
    seq, loc, _ = x.shape
    proj = wl.shape[1]
    half_res, chan = cot.shape[1], cot.shape[2]
    res = nrow * loc
    tiles = proj * seq // 128
    fr = loc * tiles
    rows = loc * seq
    lanes = loc * proj
    per_half = half_res // loc
    bres = block_rows(nrow) * loc
    hbm = pl.BlockSpec(memory_space=pltpu.HBM)
    vm = pl.BlockSpec(memory_space=pltpu.VMEM)
    operands = (x, am.T, rm.reshape(1, loc), wl.T, wr.T, w, bias.reshape(1, chan), cot)
    held = [pltpu.with_memory_space_constraint(a, pltpu.HBM) for a in operands]
    pu, lg, rg = pl.pallas_call(
        functools.partial(kernel, nrow),
        out_shape=(
            jax.ShapeDtypeStruct(cot.shape, BF16),
            jax.ShapeDtypeStruct((rows, proj), F32),
            jax.ShapeDtypeStruct((rows, proj), F32),
        ),
        in_specs=[hbm] * 8,
        out_specs=(vm, vm, vm),
        scratch_shapes=[pltpu.VMEM(a.shape, a.dtype) for a in operands]
        + [
            pltpu.VMEM((rows + seq, 128), BF16),
            pltpu.VMEM((rows + seq, 128), BF16),
            pltpu.VMEM((2, seq, lanes), BF16),
            pltpu.VMEM((nrow, 2, seq, lanes), BF16),
            pltpu.VMEM((fr, 128), BF16),
            pltpu.VMEM((nrow, fr, 128), BF16),
            pltpu.VMEM((per_half, loc * loc, chan), BF16),
            pltpu.VMEM((nrow, loc * loc, chan), BF16),
            pltpu.VMEM((loc, res, chan), BF16),
            pltpu.VMEM((1, 128), F32),
            pltpu.VMEM((2 * nrow, 1, 128), F32),
            pltpu.VMEM((proj * (proj + PAD), chan), F32),
            pltpu.VMEM((2 * half_res * tiles, 128), F32),
            pltpu.VMEM((bres * loc, chan), F32),
            pltpu.VMEM((loc * half_res, chan), F32),
            pltpu.VMEM((res, lanes), F32),
            pltpu.VMEM((proj * (bres + PAD), lanes), F32),
            pltpu.VMEM((proj * (bres + PAD), lanes), F32),
            pltpu.VMEM((bres * proj, lanes), BF16),
            pltpu.VMEM((bres * proj, lanes), BF16),
            pltpu.VMEM((loc, chan, proj * proj), BF16),
            pltpu.VMEM((2 * proj * seq, loc * chan), BF16),
            pltpu.SemaphoreType.DMA((6,)),
            pltpu.SemaphoreType.DMA((6,)),
            pltpu.SemaphoreType.DMA((8,)),
        ],
        compiler_params=pltpu.CompilerParams(
            collective_id=0, has_side_effects=True, vmem_limit_bytes=GRANT
        ),
    )(*held)
    grads = jax.ShapeDtypeStruct((rows, proj), F32)
    pu, lg, rg = pl.pallas_call(
        finish,
        out_shape=(jax.ShapeDtypeStruct(cot.shape, BF16), grads, grads),
        in_specs=[vm] * 3,
        out_specs=(vm, vm, vm),
        compiler_params=pltpu.CompilerParams(vmem_limit_bytes=GRANT),
    )(pu, lg, rg)
    return pu, lg.reshape(seq, loc, proj), rg.reshape(seq, loc, proj)


def solution(mesh):
    placed = (
        P(("grp", "col"), "row", None),
        P(("grp", "col"), "row"),
        P(("grp", "row")),
        P(),
        P(),
        P(),
        P(),
        P(("grp", "row"), "col", None),
    )
    return jax.shard_map(
        functools.partial(per_device, mesh.shape["row"]),
        mesh=mesh,
        in_specs=placed,
        out_specs=(
            P(("grp", "row"), "col", None),
            P(("grp", "col"), "row", None),
            P(("grp", "col"), "row", None),
        ),
        check_vma=False,
    )
```

```python
import functools

import jax
import jax.numpy as jnp
from jax import lax
from jax.experimental import pallas as pl
from jax.experimental.pallas import tpu as pltpu
from jax.sharding import PartitionSpec as P

F32 = jnp.float32
BF16 = jnp.bfloat16
MESH = pl.DeviceIdType.MESH
UNROLL = 8
GRANT = 40 << 20
PAD = 4


def iota(shape, axis):
    return lax.broadcasted_iota(jnp.int32, shape, axis)


def mm(a, b):
    return lax.dot_general(a, b, (((1,), (0,)), ((), ())), preferred_element_type=F32)


def mm_t(a, b):
    return lax.dot_general(a, b, (((1,), (1,)), ((), ())), preferred_element_type=F32)


def each(n, f):
    if n <= UNROLL:
        for k in range(n):
            f(k)
    else:

        @pl.loop(0, n)
        def _(k):
            f(k)


def block_rows(nrow):
    n = min(nrow, 8)
    while nrow % n:
        n -= 1
    return n


def kernel(
    nrow,
    x_hbm, am_hbm, rm_hbm, wl_hbm, wr_hbm, w_hbm, bias_hbm, cot_hbm,
    pu_ref, lg_ref, rg_ref,
    x_ref, am_ref, rm_ref, wl_ref, wr_ref, w_ref, bias_ref, cot_ref,
    g_s, g_r, n_s, n_r, f_s, f_r, ct_s, ct_r, cf_r, m_s, m_r,
    w32, a32, c32, c32b, inv_ref, og_a, og_b, k_a, k_b, wt_ref, p2,
    ssem, rsem, isem,
):
    seq, loc, feat = x_ref.shape
    proj = wl_ref.shape[0]
    half_res, chan = cot_ref.shape[1], cot_ref.shape[2]
    res = nrow * loc
    per_half = half_res // loc
    lanes = loc * proj
    tiles = proj * seq // 128
    rows = loc * seq
    lo = loc.bit_length() - 1
    sq = seq.bit_length() - 1
    tl = tiles.bit_length() - 1
    br = block_rows(nrow)
    bres = br * loc
    blocks = nrow // br

    grp, row, col = lax.axis_index("grp"), lax.axis_index("row"), lax.axis_index("col")
    other = 1 - col

    def half_of(r):
        return jnp.where(r >= per_half, 1, 0)

    def in_half(r):
        return jnp.where(r >= per_half, r - per_half, r)

    def dev(r, c):
        return (grp, r, c)

    def far_row(k):
        return jnp.where(k >= row, k + 1, k)

    loads = [
        pltpu.make_async_copy(src, dst, isem.at[k])
        for k, (src, dst) in enumerate(
            (
                (x_hbm, x_ref), (wl_hbm, wl_ref), (wr_hbm, wr_ref), (am_hbm, am_ref),
                (rm_hbm, rm_ref), (cot_hbm, cot_ref), (w_hbm, w_ref), (bias_hbm, bias_ref),
            )
        )
    ]
    for load in loads:
        load.start()

    barrier = pltpu.get_barrier_semaphore()

    def greet(k):
        r = far_row(k)
        for c in (col, other):
            pl.semaphore_signal(barrier, inc=1, device_id=dev(r, c), device_id_type=MESH)

    each(nrow - 1, greet)
    pl.semaphore_signal(barrier, inc=1, device_id=dev(row, other), device_id_type=MESH)

    group = iota((seq, 128), 1) >> (proj.bit_length() - 1)

    def pick_group(parts, lane_group):
        out = parts[0]
        for p in range(1, loc):
            out = jnp.where(lane_group == p, parts[p], out)
        return out

    for load in loads[:6]:
        load.wait()

    xf = x_ref[...].astype(F32)
    x = jnp.concatenate([xf[:, r, :] for r in range(loc)], axis=0).astype(BF16)
    pieces = [
        (am_ref[r : r + 1, :] * rm_ref[:, r : r + 1]).astype(F32) for r in range(loc)
    ]
    live = jnp.concatenate([jnp.broadcast_to(p, (seq, seq)) for p in pieces], axis=0)
    diagonal = (iota((rows, seq), 0) & (seq - 1)) == iota((rows, seq), 1)
    live = jnp.sum(jnp.where(diagonal, live, 0.0), axis=1, keepdims=True)
    live = jnp.broadcast_to(live, (rows, 128))
    lane = iota((rows, 128), 1)
    m_s[...] = jnp.sum(jnp.where(lane == iota((rows, 128), 0), live, 0.0), axis=0, keepdims=True)
    factors = jnp.concatenate([wl_ref[...]] * loc + [wr_ref[...]] * loc, axis=0)
    both = mm_t(x, factors)
    left = both[:, :lanes] * live
    right = both[:, lanes:] * live

    def natural(a):
        return pick_group([a[r * seq : (r + 1) * seq] for r in range(loc)], group)

    n_s[0] = natural(left).astype(BF16)
    n_s[1] = natural(right).astype(BF16)
    live_nat = natural(live).astype(BF16)
    g = jnp.where(lane < proj, left, live).astype(BF16)
    g_s[:rows] = g
    g_s[rows:] = live_nat

    width = proj * seq
    spread = (iota((128, width), 0) == (iota((128, width), 1) >> sq)).astype(BF16)
    own_seq = (iota((rows, width), 0) & (seq - 1)) == (iota((rows, width), 1) & (seq - 1))
    h = jnp.where(own_seq, mm(right.astype(BF16), spread), 0.0).astype(BF16)
    h = jnp.concatenate([h[:, k * 128 : (k + 1) * 128] for k in range(tiles)], axis=0)
    fr, deep = loc * tiles, tiles * rows
    fi, ki = iota((fr, deep), 0), iota((fr, deep), 1)
    f_row, f_t = fi >> tl, fi & (tiles - 1)
    k_t, k_row = ki >> (lo + sq), (ki >> sq) & (loc - 1)
    pick = ((f_row == k_row) & (f_t == k_t)).astype(BF16)
    f_s[...] = mm(pick, h).astype(BF16)

    cot32 = cot_ref[...].astype(F32)
    if per_half <= UNROLL:
        for q in range(per_half):
            ct_s[q] = jnp.concatenate(
                [cot32[i, q * loc : (q + 1) * loc, :] for i in range(loc)], axis=0
            ).astype(BF16)
    else:
        for i in range(loc):
            c32b[i * half_res : (i + 1) * half_res] = cot32[i]

        @pl.loop(0, per_half)
        def _(q):
            ct_s[q] = jnp.concatenate(
                [c32b[pl.ds(i * half_res + q * loc, loc), :] for i in range(loc)], axis=0
            ).astype(BF16)

    pl.semaphore_wait(barrier, 2 * nrow - 1)

    def copy(src, dst, kind, to):
        return pltpu.make_async_remote_copy(
            src_ref=src, dst_ref=dst, send_sem=ssem.at[kind], recv_sem=rsem.at[kind],
            device_id=to, device_id_type=MESH,
        )

    def drain(ref, count, sem):
        view = ref.at[pl.ds(0, count)]
        pltpu.make_async_copy(view, view, sem).wait()

    own_half = pl.ds(pl.multiple_of(col * half_res, half_res), half_res)
    inside = half_of(row) == col
    mine = in_half(row)

    def partner(k):
        src, dst = ((g_s, g_r), (cot_ref, cf_r.at[:, own_half, :]))[k]
        return copy(src, dst, k, dev(row, other))

    def on(pred, f):
        pl.when(pred)(f)

    def send_other(r):
        copy(m_s, m_r.at[nrow + row], 2, dev(r, other)).start()
        on(
            half_of(r) == col,
            lambda: copy(ct_s.at[in_half(r)], ct_r.at[row], 3, dev(r, other)).start(),
        )
        on(
            half_of(row) == other,
            lambda: copy(f_s, f_r.at[per_half + mine], 5, dev(r, other)).start(),
        )

    def send(k):
        r = far_row(k)
        copy(m_s, m_r.at[row], 2, dev(r, col)).start()
        on(
            half_of(r) == col,
            lambda: copy(ct_s.at[in_half(r)], ct_r.at[row], 3, dev(r, col)).start(),
        )
        copy(n_s, n_r.at[row], 4, dev(r, col)).start()
        on(inside, lambda: copy(f_s, f_r.at[mine], 5, dev(r, col)).start())
        send_other(r)

    partner(0).start()
    partner(1).start()
    each(nrow - 1, send)
    send_other(row)

    def drain_some(ref, kind, sem, less):
        on(less, lambda: drain(ref, nrow - 1, sem.at[kind]))
        on(jnp.logical_not(less), lambda: drain(ref, nrow, sem.at[kind]))

    n_r[row] = n_s[...]
    m_r[row] = m_s[...]
    cf_r[:, own_half, :] = cot_ref[...]

    @pl.when(inside)
    def _():
        ct_r[row] = ct_s[mine]
        f_r[mine] = f_s[...]

    loads[6].wait()
    loads[7].wait()
    for c in range(proj):
        w32[c * (proj + PAD) : c * (proj + PAD) + proj, :] = w_ref[
            c * proj : (c + 1) * proj, :
        ].astype(F32)
    by_e = [w32[pl.ds(e, proj, stride=proj + PAD), :].astype(BF16) for e in range(proj)]
    w_c = jnp.concatenate(by_e, axis=1)

    def turned(k, b):
        return k // loc * loc + (k % loc - b) % loc

    eye = (iota((chan, chan), 0) == iota((chan, chan), 1)).astype(BF16)
    for b in range(loc):
        order = [turned(k, b) for k in range(proj)]
        turned_w = mm_t(
            eye, jnp.concatenate([w_ref[c * proj : (c + 1) * proj, :] for c in order], axis=0)
        ).astype(BF16)
        for t in range(proj // loc):
            wt_ref[b, t] = turned_w[:, t * 128 : (t + 1) * 128]

    def spread_left(gl, part):
        p = mm(gl[:, :proj], w_c).astype(BF16)
        for e in range(proj):
            for i in range(loc):
                at = (part * proj + e) * seq
                p2[i, at : at + seq, :] = p[
                    i * seq : (i + 1) * seq, e * chan : (e + 1) * chan
                ]

    def fold(outs, dst):
        lane_group = iota((bres, 128), 1) >> (proj.bit_length() - 1)
        for t in range(proj // loc):
            part = [o[:, t * 128 : (t + 1) * 128] for o in outs]
            for k in range(loc):
                d = pick_group([part[(p - k) % loc] for p in range(loc)], lane_group)
                if k:
                    d = pltpu.roll(d, 128 - k * proj, 1)
                at = (t * loc + k) * (bres + PAD)
                dst[at : at + bres, :] = d

    def block(b):
        if isinstance(b, int):
            return pl.ds(b * bres, bres)
        return pl.ds(pl.multiple_of(b * bres, bres), bres)

    def outer_a(b):
        outs = []
        for i in range(loc):
            order = [turned(k, i) for k in range(proj)]
            outs.append(
                mm_t(cf_r[i, block(b), :], jnp.concatenate([by_e[e] for e in order], axis=0))
            )
        fold(outs, og_a)

    def outer_b(b):
        c32[...] = ct_r[pl.ds(b * br, br)].astype(F32).reshape(bres * loc, chan)
        fold(
            [
                mm(
                    c32[pl.ds(j, bres, stride=loc), :].astype(BF16),
                    jnp.concatenate([wt_ref[j, t] for t in range(proj // loc)], axis=1),
                )
                for j in range(loc)
            ],
            og_b,
        )

    def inverse(b):
        spot = (iota((bres, br), 0) >> lo == iota((bres, br), 1)).astype(BF16)
        own_lane = (iota((bres, 128), 0) & (loc - 1)) == (iota((bres, 128), 1) >> sq)
        total = None
        for k, own in enumerate((live_nat, live_other)):
            m = m_r[pl.ds(k * nrow + b * br, br)].reshape(br, 128).astype(BF16)
            m = jnp.where(own_lane, mm(spot, m), 0.0).astype(BF16)
            term = mm(m, jnp.concatenate([own] * (128 // seq), axis=0))
            total = term if total is None else total + term
        inv_ref[block(b), :] = 1.0 / jnp.maximum(total, 1.0)

    def operator(b, og, dst):
        for r in range(bres):
            dst[r * proj : (r + 1) * proj, :] = (
                og[pl.ds(r, proj, stride=bres + PAD), :] * inv_ref[pl.ds(b * bres + r, 1), :]
            ).astype(BF16)

    def grads(b, dst, k_ref, side, first):
        a = jnp.concatenate([n_r[b * br + r, side] for r in range(br)], axis=1)
        out = mm(a, k_ref[...])
        for i in range(loc):
            at = pl.ds(i, seq, stride=loc)
            part = out[:, i * proj : (i + 1) * proj]
            dst[at, :] = part if first else dst[at, :] + part

    spread_left(g, 0)
    partner(0).wait_recv()
    spread_left(g_r[:rows], 1)
    live_other = g_r[rows:]
    partner(1).wait_recv()
    if blocks == 1:
        outer_a(0)
    drain(m_r, 2 * nrow - 1, rsem.at[2])
    drain_some(ct_r, 3, rsem, inside)
    if blocks == 1:
        inverse(0)
        operator(0, og_a, k_a)
        outer_b(0)
        operator(0, og_b, k_b)
    drain(n_r, nrow - 1, rsem.at[4])
    drain_some(f_r, 5, rsem, inside)
    if blocks == 1:
        grads(0, lg_ref, k_a, 1, True)
        grads(0, rg_ref, k_b, 0, True)
    else:
        lg_ref[...] = jnp.zeros(lg_ref.shape, F32)
        rg_ref[...] = jnp.zeros(rg_ref.shape, F32)

        @pl.loop(0, blocks)
        def _(b):
            outer_a(b)
            outer_b(b)
            inverse(b)
            operator(b, og_a, k_a)
            operator(b, og_b, k_b)
            grads(b, lg_ref, k_a, 1, False)
            grads(b, rg_ref, k_b, 0, False)

    a32[...] = f_r[...].astype(F32).reshape(2 * half_res * tiles, 128)
    flat = jnp.concatenate(
        [
            a32[pl.ds(k * half_res * tiles + t, half_res, stride=tiles), :]
            for k in range(2)
            for t in range(tiles)
        ],
        axis=1,
    ).astype(BF16)
    mapped = mm(flat, jnp.concatenate([p2[i] for i in range(loc)], axis=1))
    bias = bias_ref[...]
    own_inv = inv_ref[own_half, :]
    for i in range(loc):
        inv = jnp.broadcast_to(own_inv[:, i * proj : i * proj + 1], (half_res, chan))
        pu_ref[i] = (mapped[:, i * chan : (i + 1) * chan] * inv + bias).astype(BF16)

    partner(0).wait_send()
    partner(1).wait_send()
    drain(m_r, 2 * nrow - 1, ssem.at[2])
    drain_some(ct_r, 3, ssem, inside)
    drain(n_r, nrow - 1, ssem.at[4])
    drain_some(f_r, 5, ssem, inside)


def finish(pu_in, lg_in, rg_in, pu_ref, lg_ref, rg_ref):
    pu_ref[...] = pu_in[...]
    lg_ref[...] = lg_in[...]
    rg_ref[...] = rg_in[...]


def per_device(nrow, x, am, rm, wl, wr, w, bias, cot):
    seq, loc, _ = x.shape
    proj = wl.shape[1]
    half_res, chan = cot.shape[1], cot.shape[2]
    res = nrow * loc
    tiles = proj * seq // 128
    fr = loc * tiles
    rows = loc * seq
    lanes = loc * proj
    per_half = half_res // loc
    bres = block_rows(nrow) * loc
    hbm = pl.BlockSpec(memory_space=pltpu.HBM)
    vm = pl.BlockSpec(memory_space=pltpu.VMEM)
    operands = (x, am.T, rm.reshape(1, loc), wl.T, wr.T, w, bias.reshape(1, chan), cot)
    held = [pltpu.with_memory_space_constraint(a, pltpu.HBM) for a in operands]
    pu, lg, rg = pl.pallas_call(
        functools.partial(kernel, nrow),
        out_shape=(
            jax.ShapeDtypeStruct(cot.shape, BF16),
            jax.ShapeDtypeStruct((rows, proj), F32),
            jax.ShapeDtypeStruct((rows, proj), F32),
        ),
        in_specs=[hbm] * 8,
        out_specs=(vm, vm, vm),
        scratch_shapes=[pltpu.VMEM(a.shape, a.dtype) for a in operands]
        + [
            pltpu.VMEM((rows + seq, 128), BF16),
            pltpu.VMEM((rows + seq, 128), BF16),
            pltpu.VMEM((2, seq, lanes), BF16),
            pltpu.VMEM((nrow, 2, seq, lanes), BF16),
            pltpu.VMEM((fr, 128), BF16),
            pltpu.VMEM((nrow, fr, 128), BF16),
            pltpu.VMEM((per_half, loc * loc, chan), BF16),
            pltpu.VMEM((nrow, loc * loc, chan), BF16),
            pltpu.VMEM((loc, res, chan), BF16),
            pltpu.VMEM((1, 128), F32),
            pltpu.VMEM((2 * nrow, 1, 128), F32),
            pltpu.VMEM((proj * (proj + PAD), chan), F32),
            pltpu.VMEM((2 * half_res * tiles, 128), F32),
            pltpu.VMEM((bres * loc, chan), F32),
            pltpu.VMEM((loc * half_res, chan), F32),
            pltpu.VMEM((res, lanes), F32),
            pltpu.VMEM((proj * (bres + PAD), lanes), F32),
            pltpu.VMEM((proj * (bres + PAD), lanes), F32),
            pltpu.VMEM((bres * proj, lanes), BF16),
            pltpu.VMEM((bres * proj, lanes), BF16),
            pltpu.VMEM((loc, proj // loc, chan, 128), BF16),
            pltpu.VMEM((loc, 2 * proj * seq, chan), BF16),
            pltpu.SemaphoreType.DMA((6,)),
            pltpu.SemaphoreType.DMA((6,)),
            pltpu.SemaphoreType.DMA((8,)),
        ],
        compiler_params=pltpu.CompilerParams(
            collective_id=0, has_side_effects=True, vmem_limit_bytes=GRANT
        ),
    )(*held)
    grads = jax.ShapeDtypeStruct((rows, proj), F32)
    pu, lg, rg = pl.pallas_call(
        finish,
        out_shape=(jax.ShapeDtypeStruct(cot.shape, BF16), grads, grads),
        in_specs=[vm] * 3,
        out_specs=(vm, vm, vm),
        compiler_params=pltpu.CompilerParams(vmem_limit_bytes=GRANT),
    )(pu, lg, rg)
    return pu, lg.reshape(seq, loc, proj), rg.reshape(seq, loc, proj)


def solution(mesh):
    placed = (
        P(("grp", "col"), "row", None),
        P(("grp", "col"), "row"),
        P(("grp", "row")),
        P(),
        P(),
        P(),
        P(),
        P(("grp", "row"), "col", None),
    )
    return jax.shard_map(
        functools.partial(per_device, mesh.shape["row"]),
        mesh=mesh,
        in_specs=placed,
        out_specs=(
            P(("grp", "row"), "col", None),
            P(("grp", "col"), "row", None),
            P(("grp", "col"), "row", None),
        ),
        check_vma=False,
    )
```

```python
import functools

import jax
import jax.numpy as jnp
from jax import lax
from jax.experimental import pallas as pl
from jax.experimental.pallas import tpu as pltpu
from jax.sharding import PartitionSpec as P

F32 = jnp.float32
BF16 = jnp.bfloat16
MESH = pl.DeviceIdType.MESH
UNROLL = 8
GRANT = 40 << 20
PAD = 4


def iota(shape, axis):
    return lax.broadcasted_iota(jnp.int32, shape, axis)


def mm(a, b):
    return lax.dot_general(a, b, (((1,), (0,)), ((), ())), preferred_element_type=F32)


def mm_t(a, b):
    return lax.dot_general(a, b, (((1,), (1,)), ((), ())), preferred_element_type=F32)


def each(n, f):
    if n <= UNROLL:
        for k in range(n):
            f(k)
    else:

        @pl.loop(0, n)
        def _(k):
            f(k)


def block_rows(nrow):
    n = min(nrow, 8)
    while nrow % n:
        n -= 1
    return n


def kernel(
    nrow,
    x_hbm, am_hbm, rm_hbm, wl_hbm, wr_hbm, w_hbm, bias_hbm, cot_hbm,
    pu_ref, lg_ref, rg_ref,
    x_ref, am_ref, rm_ref, wl_ref, wr_ref, w_ref, bias_ref, cot_ref,
    g_s, g_r, n_s, n_r, f_s, f_r, ct_s, ct_r, cf_r, m_s, m_r,
    w32, a32, c32, c32b, inv_ref, og_a, og_b, k_a, k_b, wt_ref, p2,
    ssem, rsem, isem,
):
    seq, loc, feat = x_ref.shape
    proj = wl_ref.shape[0]
    half_res, chan = cot_ref.shape[1], cot_ref.shape[2]
    res = nrow * loc
    per_half = half_res // loc
    lanes = loc * proj
    tiles = proj * seq // 128
    rows = loc * seq
    lo = loc.bit_length() - 1
    sq = seq.bit_length() - 1
    tl = tiles.bit_length() - 1
    br = block_rows(nrow)
    bres = br * loc
    blocks = nrow // br

    grp, row, col = lax.axis_index("grp"), lax.axis_index("row"), lax.axis_index("col")
    other = 1 - col

    def half_of(r):
        return jnp.where(r >= per_half, 1, 0)

    def in_half(r):
        return jnp.where(r >= per_half, r - per_half, r)

    def dev(r, c):
        return (grp, r, c)

    def far_row(k):
        return jnp.where(k >= row, k + 1, k)

    loads = [
        pltpu.make_async_copy(src, dst, isem.at[k])
        for k, (src, dst) in enumerate(
            (
                (x_hbm, x_ref), (wl_hbm, wl_ref), (wr_hbm, wr_ref), (am_hbm, am_ref),
                (rm_hbm, rm_ref), (cot_hbm, cot_ref), (w_hbm, w_ref), (bias_hbm, bias_ref),
            )
        )
    ]
    for load in loads:
        load.start()

    barrier = pltpu.get_barrier_semaphore()

    def greet(k):
        r = far_row(k)
        for c in (col, other):
            pl.semaphore_signal(barrier, inc=1, device_id=dev(r, c), device_id_type=MESH)

    each(nrow - 1, greet)
    pl.semaphore_signal(barrier, inc=1, device_id=dev(row, other), device_id_type=MESH)

    group = iota((seq, 128), 1) >> (proj.bit_length() - 1)

    def pick_group(parts, lane_group):
        out = parts[0]
        for p in range(1, loc):
            out = jnp.where(lane_group == p, parts[p], out)
        return out

    for load in loads[:6]:
        load.wait()

    xf = x_ref[...].astype(F32)
    x = jnp.concatenate([xf[:, r, :] for r in range(loc)], axis=0).astype(BF16)
    pieces = [
        (am_ref[r : r + 1, :] * rm_ref[:, r : r + 1]).astype(F32) for r in range(loc)
    ]
    live = jnp.concatenate([jnp.broadcast_to(p, (seq, seq)) for p in pieces], axis=0)
    diagonal = (iota((rows, seq), 0) & (seq - 1)) == iota((rows, seq), 1)
    live = jnp.sum(jnp.where(diagonal, live, 0.0), axis=1, keepdims=True)
    live = jnp.broadcast_to(live, (rows, 128))
    lane = iota((rows, 128), 1)
    m_s[...] = jnp.sum(jnp.where(lane == iota((rows, 128), 0), live, 0.0), axis=0, keepdims=True)
    factors = jnp.concatenate([wl_ref[...]] * loc + [wr_ref[...]] * loc, axis=0)
    both = mm_t(x, factors)
    left = both[:, :lanes] * live
    right = both[:, lanes:] * live

    def natural(a):
        return pick_group([a[r * seq : (r + 1) * seq] for r in range(loc)], group)

    n_s[0] = natural(left).astype(BF16)
    n_s[1] = natural(right).astype(BF16)
    live_nat = natural(live).astype(BF16)
    g = jnp.where(lane < proj, left, live).astype(BF16)
    g_s[:rows] = g
    g_s[rows:] = live_nat

    width = proj * seq
    spread = (iota((128, width), 0) == (iota((128, width), 1) >> sq)).astype(BF16)
    own_seq = (iota((rows, width), 0) & (seq - 1)) == (iota((rows, width), 1) & (seq - 1))
    h = jnp.where(own_seq, mm(right.astype(BF16), spread), 0.0).astype(BF16)
    h = jnp.concatenate([h[:, k * 128 : (k + 1) * 128] for k in range(tiles)], axis=0)
    fr, deep = loc * tiles, tiles * rows
    fi, ki = iota((fr, deep), 0), iota((fr, deep), 1)
    f_row, f_t = fi >> tl, fi & (tiles - 1)
    k_t, k_row = ki >> (lo + sq), (ki >> sq) & (loc - 1)
    pick = ((f_row == k_row) & (f_t == k_t)).astype(BF16)
    f_s[...] = mm(pick, h).astype(BF16)

    cot32 = cot_ref[...].astype(F32)
    if per_half <= UNROLL:
        for q in range(per_half):
            ct_s[q] = jnp.concatenate(
                [cot32[i, q * loc : (q + 1) * loc, :] for i in range(loc)], axis=0
            ).astype(BF16)
    else:
        for i in range(loc):
            c32b[i * half_res : (i + 1) * half_res] = cot32[i]

        @pl.loop(0, per_half)
        def _(q):
            ct_s[q] = jnp.concatenate(
                [c32b[pl.ds(i * half_res + q * loc, loc), :] for i in range(loc)], axis=0
            ).astype(BF16)

    pl.semaphore_wait(barrier, 2 * nrow - 1)

    def copy(src, dst, kind, to):
        return pltpu.make_async_remote_copy(
            src_ref=src, dst_ref=dst, send_sem=ssem.at[kind], recv_sem=rsem.at[kind],
            device_id=to, device_id_type=MESH,
        )

    def drain(ref, count, sem):
        view = ref.at[pl.ds(0, count)]
        pltpu.make_async_copy(view, view, sem).wait()

    own_half = pl.ds(pl.multiple_of(col * half_res, half_res), half_res)
    inside = half_of(row) == col
    mine = in_half(row)
    home = half_of(row)

    def partner(k):
        src, dst = ((g_s, g_r), (cot_ref, cf_r.at[:, own_half, :]))[k]
        return copy(src, dst, k, dev(row, other))

    def on(pred, f):
        pl.when(pred)(f)

    def to_both(r, near=True):
        def m(c, k):
            copy(m_s, m_r.at[k * nrow + row], 2, dev(r, c)).start()

        def ct(c, k):
            on(
                half_of(r) == col,
                lambda: copy(ct_s.at[in_half(r)], ct_r.at[row], 3, dev(r, c)).start(),
            )

        def n(c, k):
            copy(n_s, n_r.at[row], 4, dev(r, c)).start()

        def f(c, k):
            on(
                home == c,
                lambda: copy(f_s, f_r.at[k * per_half + mine], 5, dev(r, c)).start(),
            )

        for send, k in ((m, 0), (m, 1), (ct, 0), (n, 0), (ct, 1), (f, 0), (f, 1)):
            if near or k:
                send((col, other)[k], k)

    each(nrow - 1, lambda k: to_both(far_row(k)))
    to_both(row, False)
    partner(0).start()
    partner(1).start()
    def drain_some(ref, kind, sem, less):
        on(less, lambda: drain(ref, nrow - 1, sem.at[kind]))
        on(jnp.logical_not(less), lambda: drain(ref, nrow, sem.at[kind]))

    n_r[row] = n_s[...]
    m_r[row] = m_s[...]
    cf_r[:, own_half, :] = cot_ref[...]

    @pl.when(inside)
    def _():
        ct_r[row] = ct_s[mine]
        f_r[mine] = f_s[...]

    loads[6].wait()
    loads[7].wait()
    for c in range(proj):
        w32[c * (proj + PAD) : c * (proj + PAD) + proj, :] = w_ref[
            c * proj : (c + 1) * proj, :
        ].astype(F32)
    by_e = [w32[pl.ds(e, proj, stride=proj + PAD), :].astype(BF16) for e in range(proj)]
    w_c = jnp.concatenate(by_e, axis=1)

    def turned(k, b):
        return k // loc * loc + (k % loc - b) % loc

    eye = (iota((chan, chan), 0) == iota((chan, chan), 1)).astype(BF16)
    for b in range(loc):
        order = [turned(k, b) for k in range(proj)]
        turned_w = mm_t(
            eye, jnp.concatenate([w_ref[c * proj : (c + 1) * proj, :] for c in order], axis=0)
        ).astype(BF16)
        for t in range(proj // loc):
            wt_ref[b, t] = turned_w[:, t * 128 : (t + 1) * 128]

    def spread_left(gl, part):
        p = mm(gl[:, :proj], w_c).astype(BF16)
        for e in range(proj):
            for i in range(loc):
                at = (part * proj + e) * seq
                p2[i, at : at + seq, :] = p[
                    i * seq : (i + 1) * seq, e * chan : (e + 1) * chan
                ]

    def fold(outs, dst, start=0):
        n, wide = outs[0].shape
        lane_group = iota((1, 128), 1) >> (proj.bit_length() - 1)
        marks = [jnp.where(lane_group == p, 1.0, 0.0) for p in range(loc)]
        for t in range(wide // 128):
            part = [o[:, t * 128 : (t + 1) * 128] for o in outs]
            for k in range(loc):
                d = part[-k % loc] * marks[0]
                for p in range(1, loc):
                    d = d + part[(p - k) % loc] * marks[p]
                if k:
                    d = pltpu.roll(d, 128 - k * proj, 1)
                at = ((start + t) * loc + k) * (bres + PAD)
                dst[at : at + n, :] = d

    def block(b):
        if isinstance(b, int):
            return pl.ds(b * bres, bres)
        return pl.ds(pl.multiple_of(b * bres, bres), bres)

    def outer_a(b):
        outs = []
        for i in range(loc):
            order = [turned(k, i) for k in range(proj)]
            outs.append(
                mm_t(cf_r[i, block(b), :], jnp.concatenate([by_e[e] for e in order], axis=0))
            )
        fold(outs, og_a)

    def outer_b(b):
        c32[...] = ct_r[pl.ds(b * br, br)].astype(F32).reshape(bres * loc, chan)
        rows_b = [c32[pl.ds(j, bres, stride=loc), :].astype(BF16) for j in range(loc)]
        deals = proj // loc
        for t in range(0, deals, 2):
            fold(
                [
                    mm(a, jnp.concatenate([wt_ref[j, u] for u in range(t, min(t + 2, deals))], axis=1))
                    for j, a in enumerate(rows_b)
                ],
                og_b,
                t,
            )

    def inverse(b):
        spot = (iota((bres, br), 0) >> lo == iota((bres, br), 1)).astype(BF16)
        own_lane = (iota((bres, 128), 0) & (loc - 1)) == (iota((bres, 128), 1) >> sq)
        total = None
        for k, own in enumerate((live_nat, live_other)):
            m = m_r[pl.ds(k * nrow + b * br, br)].reshape(br, 128).astype(BF16)
            m = jnp.where(own_lane, mm(spot, m), 0.0).astype(BF16)
            term = mm(m, jnp.concatenate([own] * (128 // seq), axis=0))
            total = term if total is None else total + term
        inv_ref[block(b), :] = 1.0 / jnp.maximum(total, 1.0)

    def operator(b, og, dst):
        for r in range(bres):
            dst[r * proj : (r + 1) * proj, :] = (
                og[pl.ds(r, proj, stride=bres + PAD), :] * inv_ref[pl.ds(b * bres + r, 1), :]
            ).astype(BF16)

    def grads(b, dst, k_ref, side, first):
        a = jnp.concatenate([n_r[b * br + r, side] for r in range(br)], axis=1)
        out = mm(a, k_ref[...])
        for i in range(loc):
            at = pl.ds(i, seq, stride=loc)
            part = out[:, i * proj : (i + 1) * proj]
            dst[at, :] = part if first else dst[at, :] + part

    spread_left(g, 0)
    partner(0).wait_recv()
    spread_left(g_r[:rows], 1)
    live_other = g_r[rows:]
    partner(1).wait_recv()
    if blocks == 1:
        outer_a(0)
    drain(m_r, 2 * nrow - 1, rsem.at[2])
    drain_some(ct_r, 3, rsem, inside)
    if blocks == 1:
        inverse(0)
        operator(0, og_a, k_a)
        outer_b(0)
        operator(0, og_b, k_b)
    drain(n_r, nrow - 1, rsem.at[4])
    drain_some(f_r, 5, rsem, inside)
    if blocks == 1:
        grads(0, lg_ref, k_a, 1, True)
        grads(0, rg_ref, k_b, 0, True)
    else:
        lg_ref[...] = jnp.zeros(lg_ref.shape, F32)
        rg_ref[...] = jnp.zeros(rg_ref.shape, F32)

        @pl.loop(0, blocks)
        def _(b):
            outer_a(b)
            outer_b(b)
            inverse(b)
            operator(b, og_a, k_a)
            operator(b, og_b, k_b)
            grads(b, lg_ref, k_a, 1, False)
            grads(b, rg_ref, k_b, 0, False)

    a32[...] = f_r[...].astype(F32).reshape(2 * half_res * tiles, 128)
    flat = jnp.concatenate(
        [
            a32[pl.ds(k * half_res * tiles + t, half_res, stride=tiles), :]
            for k in range(2)
            for t in range(tiles)
        ],
        axis=1,
    ).astype(BF16)
    mapped = mm(flat, jnp.concatenate([p2[i] for i in range(loc)], axis=1))
    bias = bias_ref[...]
    own_inv = inv_ref[own_half, :]
    for i in range(loc):
        inv = jnp.broadcast_to(own_inv[:, i * proj : i * proj + 1], (half_res, chan))
        pu_ref[i] = (mapped[:, i * chan : (i + 1) * chan] * inv + bias).astype(BF16)

    partner(0).wait_send()
    partner(1).wait_send()
    drain(m_r, 2 * nrow - 1, ssem.at[2])
    drain_some(ct_r, 3, ssem, inside)
    drain(n_r, nrow - 1, ssem.at[4])
    drain_some(f_r, 5, ssem, inside)


def finish(pu_in, lg_in, rg_in, pu_ref, lg_ref, rg_ref):
    pu_ref[...] = pu_in[...]
    lg_ref[...] = lg_in[...]
    rg_ref[...] = rg_in[...]


def per_device(nrow, x, am, rm, wl, wr, w, bias, cot):
    seq, loc, _ = x.shape
    proj = wl.shape[1]
    half_res, chan = cot.shape[1], cot.shape[2]
    res = nrow * loc
    tiles = proj * seq // 128
    fr = loc * tiles
    rows = loc * seq
    lanes = loc * proj
    per_half = half_res // loc
    bres = block_rows(nrow) * loc
    hbm = pl.BlockSpec(memory_space=pltpu.HBM)
    vm = pl.BlockSpec(memory_space=pltpu.VMEM)
    operands = (x, am.T, rm.reshape(1, loc), wl.T, wr.T, w, bias.reshape(1, chan), cot)
    held = [pltpu.with_memory_space_constraint(a, pltpu.HBM) for a in operands]
    pu, lg, rg = pl.pallas_call(
        functools.partial(kernel, nrow),
        out_shape=(
            jax.ShapeDtypeStruct(cot.shape, BF16),
            jax.ShapeDtypeStruct((rows, proj), F32),
            jax.ShapeDtypeStruct((rows, proj), F32),
        ),
        in_specs=[hbm] * 8,
        out_specs=(vm, vm, vm),
        scratch_shapes=[pltpu.VMEM(a.shape, a.dtype) for a in operands]
        + [
            pltpu.VMEM((rows + seq, 128), BF16),
            pltpu.VMEM((rows + seq, 128), BF16),
            pltpu.VMEM((2, seq, lanes), BF16),
            pltpu.VMEM((nrow, 2, seq, lanes), BF16),
            pltpu.VMEM((fr, 128), BF16),
            pltpu.VMEM((nrow, fr, 128), BF16),
            pltpu.VMEM((per_half, loc * loc, chan), BF16),
            pltpu.VMEM((nrow, loc * loc, chan), BF16),
            pltpu.VMEM((loc, res, chan), BF16),
            pltpu.VMEM((1, 128), F32),
            pltpu.VMEM((2 * nrow, 1, 128), F32),
            pltpu.VMEM((proj * (proj + PAD), chan), F32),
            pltpu.VMEM((2 * half_res * tiles, 128), F32),
            pltpu.VMEM((bres * loc, chan), F32),
            pltpu.VMEM((loc * half_res, chan), F32),
            pltpu.VMEM((res, lanes), F32),
            pltpu.VMEM((proj * (bres + PAD), lanes), F32),
            pltpu.VMEM((proj * (bres + PAD), lanes), F32),
            pltpu.VMEM((bres * proj, lanes), BF16),
            pltpu.VMEM((bres * proj, lanes), BF16),
            pltpu.VMEM((loc, proj // loc, chan, 128), BF16),
            pltpu.VMEM((loc, 2 * proj * seq, chan), BF16),
            pltpu.SemaphoreType.DMA((6,)),
            pltpu.SemaphoreType.DMA((6,)),
            pltpu.SemaphoreType.DMA((8,)),
        ],
        compiler_params=pltpu.CompilerParams(
            collective_id=0, has_side_effects=True, vmem_limit_bytes=GRANT
        ),
    )(*held)
    grads = jax.ShapeDtypeStruct((rows, proj), F32)
    pu, lg, rg = pl.pallas_call(
        finish,
        out_shape=(jax.ShapeDtypeStruct(cot.shape, BF16), grads, grads),
        in_specs=[vm] * 3,
        out_specs=(vm, vm, vm),
        compiler_params=pltpu.CompilerParams(vmem_limit_bytes=GRANT),
    )(pu, lg, rg)
    return pu, lg.reshape(seq, loc, proj), rg.reshape(seq, loc, proj)


def solution(mesh):
    placed = (
        P(("grp", "col"), "row", None),
        P(("grp", "col"), "row"),
        P(("grp", "row")),
        P(),
        P(),
        P(),
        P(),
        P(("grp", "row"), "col", None),
    )
    return jax.shard_map(
        functools.partial(per_device, mesh.shape["row"]),
        mesh=mesh,
        in_specs=placed,
        out_specs=(
            P(("grp", "row"), "col", None),
            P(("grp", "col"), "row", None),
            P(("grp", "col"), "row", None),
        ),
        check_vma=False,
    )
```

```python
import functools

import jax
import jax.numpy as jnp
from jax import lax
from jax.experimental import pallas as pl
from jax.experimental.pallas import tpu as pltpu
from jax.sharding import PartitionSpec as P

F32 = jnp.float32
BF16 = jnp.bfloat16
MESH = pl.DeviceIdType.MESH
UNROLL = 8
GRANT = 40 << 20
PAD = 4


def iota(shape, axis):
    return lax.broadcasted_iota(jnp.int32, shape, axis)


def mm(a, b):
    return lax.dot_general(a, b, (((1,), (0,)), ((), ())), preferred_element_type=F32)


def mm_t(a, b):
    return lax.dot_general(a, b, (((1,), (1,)), ((), ())), preferred_element_type=F32)


def each(n, f):
    if n <= UNROLL:
        for k in range(n):
            f(k)
    else:

        @pl.loop(0, n)
        def _(k):
            f(k)


def block_rows(nrow):
    n = min(nrow, 8)
    while nrow % n:
        n -= 1
    return n


def kernel(
    nrow,
    x_hbm, am_hbm, rm_hbm, wl_hbm, wr_hbm, w_hbm, bias_hbm, cot_hbm,
    pu_ref, lg_ref, rg_ref,
    x_ref, am_ref, rm_ref, wl_ref, wr_ref, w_ref, bias_ref, cot_ref,
    g_s, g_r, n_s, n_r, f_s, f_r, ct_s, ct_r, cf_r, m_s, m_r,
    w32, a32, c32, c32b, inv_ref, raw_a, acc_ref, k_a, k_b, wt_ref, p2,
    ssem, rsem, isem,
):
    seq, loc, feat = x_ref.shape
    proj = wl_ref.shape[0]
    half_res, chan = cot_ref.shape[1], cot_ref.shape[2]
    res = nrow * loc
    per_half = half_res // loc
    lanes = loc * proj
    tiles = proj * seq // 128
    rows = loc * seq
    lo = loc.bit_length() - 1
    sq = seq.bit_length() - 1
    tl = tiles.bit_length() - 1
    br = block_rows(nrow)
    bres = br * loc
    blocks = nrow // br
    deals = proj // loc
    lot = 2 * deals * loc

    grp, row, col = lax.axis_index("grp"), lax.axis_index("row"), lax.axis_index("col")
    other = 1 - col

    def half_of(r):
        return jnp.where(r >= per_half, 1, 0)

    def in_half(r):
        return jnp.where(r >= per_half, r - per_half, r)

    def dev(r, c):
        return (grp, r, c)

    def far_row(k):
        return jnp.where(k >= row, k + 1, k)

    loads = [
        pltpu.make_async_copy(src, dst, isem.at[k])
        for k, (src, dst) in enumerate(
            (
                (x_hbm, x_ref), (wl_hbm, wl_ref), (wr_hbm, wr_ref), (am_hbm, am_ref),
                (rm_hbm, rm_ref), (cot_hbm, cot_ref), (w_hbm, w_ref), (bias_hbm, bias_ref),
            )
        )
    ]
    for load in loads:
        load.start()

    barrier = pltpu.get_barrier_semaphore()

    def greet(k):
        r = far_row(k)
        for c in (col, other):
            pl.semaphore_signal(barrier, inc=1, device_id=dev(r, c), device_id_type=MESH)

    each(nrow - 1, greet)
    pl.semaphore_signal(barrier, inc=1, device_id=dev(row, other), device_id_type=MESH)

    group = iota((seq, 128), 1) >> (proj.bit_length() - 1)

    def pick_group(parts, lane_group):
        out = parts[0]
        for p in range(1, loc):
            out = jnp.where(lane_group == p, parts[p], out)
        return out

    for load in loads[:6]:
        load.wait()

    xf = x_ref[...].astype(F32)
    x = jnp.concatenate([xf[:, r, :] for r in range(loc)], axis=0).astype(BF16)
    pieces = [
        (am_ref[r : r + 1, :] * rm_ref[:, r : r + 1]).astype(F32) for r in range(loc)
    ]
    live = jnp.concatenate([jnp.broadcast_to(p, (seq, seq)) for p in pieces], axis=0)
    diagonal = (iota((rows, seq), 0) & (seq - 1)) == iota((rows, seq), 1)
    live = jnp.sum(jnp.where(diagonal, live, 0.0), axis=1, keepdims=True)
    live = jnp.broadcast_to(live, (rows, 128))
    lane = iota((rows, 128), 1)
    m_s[...] = jnp.sum(jnp.where(lane == iota((rows, 128), 0), live, 0.0), axis=0, keepdims=True)
    factors = jnp.concatenate([wl_ref[...]] * loc + [wr_ref[...]] * loc, axis=0)
    both = mm_t(x, factors)
    left = both[:, :lanes] * live
    right = both[:, lanes:] * live

    def natural(a):
        return pick_group([a[r * seq : (r + 1) * seq] for r in range(loc)], group)

    n_s[0] = natural(left).astype(BF16)
    n_s[1] = natural(right).astype(BF16)
    g = left.astype(BF16)
    live_b = live.astype(BF16)
    g_s[:rows] = g
    g_s[rows:] = live_b

    width = proj * seq
    spread = (iota((128, width), 0) == (iota((128, width), 1) >> sq)).astype(BF16)
    own_seq = (iota((rows, width), 0) & (seq - 1)) == (iota((rows, width), 1) & (seq - 1))
    h = jnp.where(own_seq, mm(right.astype(BF16), spread), 0.0).astype(BF16)
    h = jnp.concatenate([h[:, k * 128 : (k + 1) * 128] for k in range(tiles)], axis=0)
    fr, deep = loc * tiles, tiles * rows
    fi, ki = iota((fr, deep), 0), iota((fr, deep), 1)
    f_row, f_t = fi >> tl, fi & (tiles - 1)
    k_t, k_row = ki >> (lo + sq), (ki >> sq) & (loc - 1)
    pick = ((f_row == k_row) & (f_t == k_t)).astype(BF16)
    f_s[...] = mm(pick, h).astype(BF16)

    cot32 = cot_ref[...].astype(F32)
    if per_half <= UNROLL:
        for q in range(per_half):
            ct_s[q] = jnp.concatenate(
                [cot32[i, q * loc : (q + 1) * loc, :] for i in range(loc)], axis=0
            ).astype(BF16)
    else:
        for i in range(loc):
            c32b[i * half_res : (i + 1) * half_res] = cot32[i]

        @pl.loop(0, per_half)
        def _(q):
            ct_s[q] = jnp.concatenate(
                [c32b[pl.ds(i * half_res + q * loc, loc), :] for i in range(loc)], axis=0
            ).astype(BF16)

    pl.semaphore_wait(barrier, 2 * nrow - 1)

    def copy(src, dst, kind, to):
        return pltpu.make_async_remote_copy(
            src_ref=src, dst_ref=dst, send_sem=ssem.at[kind], recv_sem=rsem.at[kind],
            device_id=to, device_id_type=MESH,
        )

    def drain(ref, count, sem):
        view = ref.at[pl.ds(0, count)]
        pltpu.make_async_copy(view, view, sem).wait()

    own_half = pl.ds(pl.multiple_of(col * half_res, half_res), half_res)
    inside = half_of(row) == col
    mine = in_half(row)

    def partner(k):
        src, dst = ((g_s, g_r), (cot_ref, cf_r.at[:, own_half, :]))[k]
        return copy(src, dst, k, dev(row, other))

    def on(pred, f):
        pl.when(pred)(f)

    def send_other(r):
        copy(m_s, m_r.at[nrow + row], 2, dev(r, other)).start()
        on(
            half_of(r) == col,
            lambda: copy(ct_s.at[in_half(r)], ct_r.at[row], 3, dev(r, other)).start(),
        )
        on(
            half_of(row) == other,
            lambda: copy(f_s, f_r.at[per_half + mine], 5, dev(r, other)).start(),
        )

    def send(k):
        r = far_row(k)
        copy(m_s, m_r.at[row], 2, dev(r, col)).start()
        on(
            half_of(r) == col,
            lambda: copy(ct_s.at[in_half(r)], ct_r.at[row], 3, dev(r, col)).start(),
        )
        copy(n_s, n_r.at[row], 4, dev(r, col)).start()
        on(inside, lambda: copy(f_s, f_r.at[mine], 5, dev(r, col)).start())
        send_other(r)

    partner(0).start()
    partner(1).start()
    each(nrow - 1, send)
    send_other(row)

    def drain_some(ref, kind, sem, less):
        on(less, lambda: drain(ref, nrow - 1, sem.at[kind]))
        on(jnp.logical_not(less), lambda: drain(ref, nrow, sem.at[kind]))

    n_r[row] = n_s[...]
    m_r[row] = m_s[...]
    cf_r[:, own_half, :] = cot_ref[...]

    @pl.when(inside)
    def _():
        ct_r[row] = ct_s[mine]
        f_r[mine] = f_s[...]

    loads[6].wait()
    loads[7].wait()
    for c in range(proj):
        w32[c * (proj + PAD) : c * (proj + PAD) + proj, :] = w_ref[
            c * proj : (c + 1) * proj, :
        ].astype(F32)
    by_e = [w32[pl.ds(e, proj, stride=proj + PAD), :].astype(BF16) for e in range(proj)]
    w_c = jnp.concatenate(by_e, axis=1)

    eye = (iota((chan, chan), 0) == iota((chan, chan), 1)).astype(BF16)
    across = mm_t(eye, w_ref[...]).astype(BF16)
    for t in range(deals):
        wt_ref[t] = across[:, t * 128 : (t + 1) * 128]

    def spread_left(gl, part):
        p = mm(gl[:, :proj], w_c).astype(BF16)
        for e in range(proj):
            for i in range(loc):
                at = (part * proj + e) * seq
                p2[i, at : at + seq, :] = p[
                    i * seq : (i + 1) * seq, e * chan : (e + 1) * chan
                ]

    def block(b):
        if isinstance(b, int):
            return pl.ds(b * bres, bres)
        return pl.ds(pl.multiple_of(b * bres, bres), bres)

    def outer_a(b):
        a = jnp.concatenate([cf_r[i, block(b), :] for i in range(loc)], axis=0)
        return mm_t(a, jnp.concatenate(by_e, axis=0))

    def outer_b(b):
        c32[...] = ct_r[pl.ds(b * br, br)].astype(F32).reshape(bres * loc, chan)
        a = jnp.concatenate([c32[pl.ds(j, bres, stride=loc), :] for j in range(loc)], axis=0)
        return mm(a.astype(BF16), jnp.concatenate([wt_ref[t] for t in range(deals)], axis=1))

    spot = (iota((bres, br), 0) >> lo == iota((bres, br), 1)).astype(BF16)
    own_lane = (iota((bres, 128), 0) & (loc - 1)) == (iota((bres, 128), 1) >> sq)

    def inverse(b):
        m = jnp.concatenate(
            [
                jnp.where(
                    own_lane,
                    mm(spot, m_r[pl.ds(k * nrow + b * br, br)].reshape(br, 128).astype(BF16)),
                    0.0,
                ).astype(BF16)
                for k in range(2)
            ],
            axis=1,
        )
        total = mm(m, lives)
        inv = 1.0 / jnp.maximum(total, 1.0)
        for i in range(loc):
            inv_ref[i, block(b), :] = inv[:, i * 128 : (i + 1) * 128]

    def operator(b, i, tile, dst):
        dst[i] = jnp.concatenate(
            [
                tile(t)[v * 2 * loc : (v + 1) * 2 * loc]
                * inv_ref[i, pl.ds(b * bres + v * 2 * loc, 2 * loc), :]
                for v in range(br // 2)
                for t in range(deals)
            ],
            axis=0,
        ).astype(BF16)

    def piece(out, i, t):
        return out[i * bres : (i + 1) * bres, t * 128 : (t + 1) * 128]

    ei, ej = iota((2 * lanes, lot * loc), 0), iota((2 * lanes, lot * loc), 1)
    pj = proj.bit_length() - 1
    de = deals.bit_length() - 1
    e_res, e_chan = ei >> pj, ei & (proj - 1)
    j_res = ej & (2 * loc - 1)
    j_deal = (ej >> (lo + 1)) & (deals - 1)
    j_class = ej >> (lo + 1 + de)
    expand = ((e_res == j_res) & (e_chan == j_deal * loc + j_class)).astype(BF16)

    def spread_blocks(b):
        a = jnp.concatenate(
            [
                jnp.concatenate([n_r[b * br + 2 * v, side], n_r[b * br + 2 * v + 1, side]], axis=1)
                for side in range(2)
                for v in range(br // 2)
            ],
            axis=0,
        )
        a = mm(a, expand).astype(BF16)

        def part(side, v, k):
            at = (side * (br // 2) + v) * seq
            return a[at : at + seq, k * lot : (k + 1) * lot]

        return [
            jnp.concatenate(
                [
                    jnp.concatenate([part(side, v, k) for v in range(br // 2)], axis=1)
                    for k in range(loc)
                ],
                axis=0,
            ).astype(BF16)
            for side in range(2)
        ]

    def grads(b, emit):
        sides = spread_blocks(b)
        for side, k_ref in ((1, k_a), (0, k_b)):
            for i in range(loc):
                if i % 2 == 0:
                    last = min(i + 2, loc)
                    pair = mm(
                        sides[side], jnp.concatenate([k_ref[k] for k in range(i, last)], axis=1)
                    )
                y = pair[:, i % 2 * 128 : (i % 2 + 1) * 128]
                total = y[:seq, :proj]
                for p in range(1, loc):
                    total = total + y[p * seq : (p + 1) * seq, p * proj : (p + 1) * proj]
                emit(side, i, total)

    spread_left(g, 0)
    partner(0).wait_recv()
    spread_left(g_r[:rows], 1)

    def live_columns(live_rows):
        return jnp.concatenate(
            [
                jnp.concatenate([live_rows[i * seq : (i + 1) * seq]] * (128 // seq), axis=0)
                for i in range(loc)
            ],
            axis=1,
        )

    lives = jnp.concatenate([live_columns(live_b), live_columns(g_r[rows:])], axis=0)
    partner(1).wait_recv()

    def signs():
        drain(m_r, 2 * nrow - 1, rsem.at[2])
        drain_some(ct_r, 3, rsem, inside)

    if blocks == 1:
        out = outer_a(0)
        for i in range(loc):
            for t in range(deals):
                raw_a[i, t] = piece(out, i, t)
        signs()
        inverse(0)
        outs = outer_b(0)
        for i in range(loc):
            operator(0, i, lambda t: raw_a[i, t], k_a)
        for i in range(loc):
            operator(0, i, lambda t: piece(outs, i, t), k_b)
        drain(n_r, nrow - 1, rsem.at[4])
        drain_some(f_r, 5, rsem, inside)

        def emit(side, i, y):
            (rg_ref, lg_ref)[side][pl.ds(i, seq, stride=loc), :] = y

        grads(0, emit)
    else:
        signs()
        drain(n_r, nrow - 1, rsem.at[4])
        drain_some(f_r, 5, rsem, inside)
        acc_ref[...] = jnp.zeros(acc_ref.shape, F32)

        @pl.loop(0, blocks)
        def _(b):
            inverse(b)
            outs = outer_b(b)
            out = outer_a(b)
            for i in range(loc):
                operator(b, i, lambda t: piece(out, i, t), k_a)
                operator(b, i, lambda t: piece(outs, i, t), k_b)

            def emit(side, i, y):
                acc_ref[side, i, :, :proj] += y

            grads(b, emit)

        for side, dst in ((1, lg_ref), (0, rg_ref)):
            for i in range(loc):
                dst[pl.ds(i, seq, stride=loc), :] = acc_ref[side, i, :, :proj]

    a32[...] = f_r[...].astype(F32).reshape(2 * half_res * tiles, 128)
    flat = jnp.concatenate(
        [
            a32[pl.ds(k * half_res * tiles + t, half_res, stride=tiles), :]
            for k in range(2)
            for t in range(tiles)
        ],
        axis=1,
    ).astype(BF16)
    mapped = mm(flat, jnp.concatenate([p2[i] for i in range(loc)], axis=1))
    bias = bias_ref[...]
    for i in range(loc):
        inv = inv_ref[i, own_half, :]
        pu_ref[i] = (mapped[:, i * chan : (i + 1) * chan] * inv + bias).astype(BF16)

    partner(0).wait_send()
    partner(1).wait_send()
    drain(m_r, 2 * nrow - 1, ssem.at[2])
    drain_some(ct_r, 3, ssem, inside)
    drain(n_r, nrow - 1, ssem.at[4])
    drain_some(f_r, 5, ssem, inside)


def finish(pu_in, lg_in, rg_in, pu_ref, lg_ref, rg_ref):
    pu_ref[...] = pu_in[...]
    lg_ref[...] = lg_in[...]
    rg_ref[...] = rg_in[...]


def per_device(nrow, x, am, rm, wl, wr, w, bias, cot):
    seq, loc, _ = x.shape
    proj = wl.shape[1]
    half_res, chan = cot.shape[1], cot.shape[2]
    res = nrow * loc
    tiles = proj * seq // 128
    fr = loc * tiles
    rows = loc * seq
    lanes = loc * proj
    per_half = half_res // loc
    bres = block_rows(nrow) * loc
    hbm = pl.BlockSpec(memory_space=pltpu.HBM)
    vm = pl.BlockSpec(memory_space=pltpu.VMEM)
    operands = (x, am.T, rm.reshape(1, loc), wl.T, wr.T, w, bias.reshape(1, chan), cot)
    held = [pltpu.with_memory_space_constraint(a, pltpu.HBM) for a in operands]
    pu, lg, rg = pl.pallas_call(
        functools.partial(kernel, nrow),
        out_shape=(
            jax.ShapeDtypeStruct(cot.shape, BF16),
            jax.ShapeDtypeStruct((rows, proj), F32),
            jax.ShapeDtypeStruct((rows, proj), F32),
        ),
        in_specs=[hbm] * 8,
        out_specs=(vm, vm, vm),
        scratch_shapes=[pltpu.VMEM(a.shape, a.dtype) for a in operands]
        + [
            pltpu.VMEM((2 * rows, 128), BF16),
            pltpu.VMEM((2 * rows, 128), BF16),
            pltpu.VMEM((2, seq, lanes), BF16),
            pltpu.VMEM((nrow, 2, seq, lanes), BF16),
            pltpu.VMEM((fr, 128), BF16),
            pltpu.VMEM((nrow, fr, 128), BF16),
            pltpu.VMEM((per_half, loc * loc, chan), BF16),
            pltpu.VMEM((nrow, loc * loc, chan), BF16),
            pltpu.VMEM((loc, res, chan), BF16),
            pltpu.VMEM((1, 128), F32),
            pltpu.VMEM((2 * nrow, 1, 128), F32),
            pltpu.VMEM((proj * (proj + PAD), chan), F32),
            pltpu.VMEM((2 * half_res * tiles, 128), F32),
            pltpu.VMEM((bres * loc, chan), F32),
            pltpu.VMEM((loc * half_res, chan), F32),
            pltpu.VMEM((loc, res, 128), F32),
            pltpu.VMEM((loc, proj // loc, bres, 128), F32),
            pltpu.VMEM((2, loc, seq, 128), F32),
            pltpu.VMEM((loc, bres * (proj // loc), 128), BF16),
            pltpu.VMEM((loc, bres * (proj // loc), 128), BF16),
            pltpu.VMEM((proj // loc, chan, 128), BF16),
            pltpu.VMEM((loc, 2 * proj * seq, chan), BF16),
            pltpu.SemaphoreType.DMA((6,)),
            pltpu.SemaphoreType.DMA((6,)),
            pltpu.SemaphoreType.DMA((8,)),
        ],
        compiler_params=pltpu.CompilerParams(
            collective_id=0, has_side_effects=True, vmem_limit_bytes=GRANT
        ),
    )(*held)
    grads = jax.ShapeDtypeStruct((rows, proj), F32)
    pu, lg, rg = pl.pallas_call(
        finish,
        out_shape=(jax.ShapeDtypeStruct(cot.shape, BF16), grads, grads),
        in_specs=[vm] * 3,
        out_specs=(vm, vm, vm),
        compiler_params=pltpu.CompilerParams(vmem_limit_bytes=GRANT),
    )(pu, lg, rg)
    return pu, lg.reshape(seq, loc, proj), rg.reshape(seq, loc, proj)


def solution(mesh):
    placed = (
        P(("grp", "col"), "row", None),
        P(("grp", "col"), "row"),
        P(("grp", "row")),
        P(),
        P(),
        P(),
        P(),
        P(("grp", "row"), "col", None),
    )
    return jax.shard_map(
        functools.partial(per_device, mesh.shape["row"]),
        mesh=mesh,
        in_specs=placed,
        out_specs=(
            P(("grp", "row"), "col", None),
            P(("grp", "col"), "row", None),
            P(("grp", "col"), "row", None),
        ),
        check_vma=False,
    )
```

```python
import functools

import jax
import jax.numpy as jnp
from jax import lax
from jax.experimental import pallas as pl
from jax.experimental.pallas import tpu as pltpu
from jax.sharding import PartitionSpec as P

F32 = jnp.float32
BF16 = jnp.bfloat16
MESH = pl.DeviceIdType.MESH
UNROLL = 8
GRANT = 40 << 20
PAD = 4


def iota(shape, axis):
    return lax.broadcasted_iota(jnp.int32, shape, axis)


def mm(a, b):
    return lax.dot_general(a, b, (((1,), (0,)), ((), ())), preferred_element_type=F32)


def mm_t(a, b):
    return lax.dot_general(a, b, (((1,), (1,)), ((), ())), preferred_element_type=F32)


def each(n, f):
    if n <= UNROLL:
        for k in range(n):
            f(k)
    else:

        @pl.loop(0, n)
        def _(k):
            f(k)


def block_rows(nrow):
    n = min(nrow, 8)
    while nrow % n:
        n -= 1
    return n


def kernel(
    nrow,
    x_hbm, am_hbm, rm_hbm, wl_hbm, wr_hbm, w_hbm, bias_hbm, cot_hbm,
    pu_ref, lg_ref, rg_ref,
    x_ref, am_ref, rm_ref, wl_ref, wr_ref, w_ref, bias_ref, cot_ref,
    g_s, g_r, n_s, n_r, f_s, f_r, ct_s, ct_r, cf_r, m_s, m_r,
    w32, a32, c32, c32b, inv_ref, og_a, og_b, k_a, k_b, wt_ref, p2,
    ssem, rsem, isem,
):
    seq, loc, feat = x_ref.shape
    proj = wl_ref.shape[0]
    half_res, chan = cot_ref.shape[1], cot_ref.shape[2]
    res = nrow * loc
    per_half = half_res // loc
    lanes = loc * proj
    tiles = proj * seq // 128
    rows = loc * seq
    lo = loc.bit_length() - 1
    sq = seq.bit_length() - 1
    tl = tiles.bit_length() - 1
    br = block_rows(nrow)
    bres = br * loc
    blocks = nrow // br

    grp, row, col = lax.axis_index("grp"), lax.axis_index("row"), lax.axis_index("col")
    other = 1 - col

    def half_of(r):
        return jnp.where(r >= per_half, 1, 0)

    def in_half(r):
        return jnp.where(r >= per_half, r - per_half, r)

    def dev(r, c):
        return (grp, r, c)

    def far_row(k):
        return jnp.where(k >= row, k + 1, k)

    loads = [
        pltpu.make_async_copy(src, dst, isem.at[k])
        for k, (src, dst) in enumerate(
            (
                (x_hbm, x_ref), (wl_hbm, wl_ref), (wr_hbm, wr_ref), (am_hbm, am_ref),
                (rm_hbm, rm_ref), (cot_hbm, cot_ref), (w_hbm, w_ref), (bias_hbm, bias_ref),
            )
        )
    ]
    for load in loads:
        load.start()

    barrier = pltpu.get_barrier_semaphore()

    def greet(k):
        r = far_row(k)
        for c in (col, other):
            pl.semaphore_signal(barrier, inc=1, device_id=dev(r, c), device_id_type=MESH)

    each(nrow - 1, greet)
    pl.semaphore_signal(barrier, inc=1, device_id=dev(row, other), device_id_type=MESH)

    group = iota((seq, 128), 1) >> (proj.bit_length() - 1)

    def pick_group(parts, lane_group):
        out = parts[0]
        for p in range(1, loc):
            out = jnp.where(lane_group == p, parts[p], out)
        return out

    for load in loads[:6]:
        load.wait()

    xf = x_ref[...].astype(F32)
    x = jnp.concatenate([xf[:, r, :] for r in range(loc)], axis=0).astype(BF16)
    pieces = [
        (am_ref[r : r + 1, :] * rm_ref[:, r : r + 1]).astype(F32) for r in range(loc)
    ]
    live = jnp.concatenate([jnp.broadcast_to(p, (seq, seq)) for p in pieces], axis=0)
    diagonal = (iota((rows, seq), 0) & (seq - 1)) == iota((rows, seq), 1)
    live = jnp.sum(jnp.where(diagonal, live, 0.0), axis=1, keepdims=True)
    live = jnp.broadcast_to(live, (rows, 128))
    lane = iota((rows, 128), 1)
    m_s[...] = jnp.sum(jnp.where(lane == iota((rows, 128), 0), live, 0.0), axis=0, keepdims=True)
    factors = jnp.concatenate([wl_ref[...]] * loc + [wr_ref[...]] * loc, axis=0)
    both = mm_t(x, factors)
    left = both[:, :lanes] * live
    right = both[:, lanes:] * live

    def natural(a):
        return pick_group([a[r * seq : (r + 1) * seq] for r in range(loc)], group)

    n_s[0] = natural(left).astype(BF16)
    n_s[1] = natural(right).astype(BF16)
    live_nat = natural(live).astype(BF16)
    g = jnp.where(lane < proj, left, live).astype(BF16)
    g_s[:rows] = g
    g_s[rows:] = live_nat

    width = proj * seq
    spread = (iota((128, width), 0) == (iota((128, width), 1) >> sq)).astype(BF16)
    own_seq = (iota((rows, width), 0) & (seq - 1)) == (iota((rows, width), 1) & (seq - 1))
    h = jnp.where(own_seq, mm(right.astype(BF16), spread), 0.0).astype(BF16)
    h = jnp.concatenate([h[:, k * 128 : (k + 1) * 128] for k in range(tiles)], axis=0)
    fr, deep = loc * tiles, tiles * rows
    fi, ki = iota((fr, deep), 0), iota((fr, deep), 1)
    f_row, f_t = fi >> tl, fi & (tiles - 1)
    k_t, k_row = ki >> (lo + sq), (ki >> sq) & (loc - 1)
    pick = ((f_row == k_row) & (f_t == k_t)).astype(BF16)
    f_s[...] = mm(pick, h).astype(BF16)

    cot32 = cot_ref[...].astype(F32)
    if per_half <= UNROLL:
        for q in range(per_half):
            ct_s[q] = jnp.concatenate(
                [cot32[i, q * loc : (q + 1) * loc, :] for i in range(loc)], axis=0
            ).astype(BF16)
    else:
        for i in range(loc):
            c32b[i * half_res : (i + 1) * half_res] = cot32[i]

        @pl.loop(0, per_half)
        def _(q):
            ct_s[q] = jnp.concatenate(
                [c32b[pl.ds(i * half_res + q * loc, loc), :] for i in range(loc)], axis=0
            ).astype(BF16)

    pl.semaphore_wait(barrier, 2 * nrow - 1)

    def copy(src, dst, kind, to):
        return pltpu.make_async_remote_copy(
            src_ref=src, dst_ref=dst, send_sem=ssem.at[kind], recv_sem=rsem.at[kind],
            device_id=to, device_id_type=MESH,
        )

    def drain(ref, count, sem):
        view = ref.at[pl.ds(0, count)]
        pltpu.make_async_copy(view, view, sem).wait()

    own_half = pl.ds(pl.multiple_of(col * half_res, half_res), half_res)
    inside = half_of(row) == col
    mine = in_half(row)

    def partner(k):
        src, dst = ((g_s, g_r), (cot_ref, cf_r.at[:, own_half, :]))[k]
        return copy(src, dst, k, dev(row, other))

    def on(pred, f):
        pl.when(pred)(f)

    def send_other(r):
        copy(m_s, m_r.at[nrow + row], 2, dev(r, other)).start()
        on(
            half_of(r) == col,
            lambda: copy(ct_s.at[in_half(r)], ct_r.at[row], 3, dev(r, other)).start(),
        )
        on(
            half_of(row) == other,
            lambda: copy(f_s, f_r.at[per_half + mine], 5, dev(r, other)).start(),
        )

    def send(k):
        r = far_row(k)
        copy(m_s, m_r.at[row], 2, dev(r, col)).start()
        on(
            half_of(r) == col,
            lambda: copy(ct_s.at[in_half(r)], ct_r.at[row], 3, dev(r, col)).start(),
        )
        copy(n_s, n_r.at[row], 4, dev(r, col)).start()
        send_other(r)
        on(inside, lambda: copy(f_s, f_r.at[mine], 5, dev(r, col)).start())

    partner(0).start()
    partner(1).start()
    each(nrow - 1, send)
    send_other(row)

    def drain_some(ref, kind, sem, less):
        on(less, lambda: drain(ref, nrow - 1, sem.at[kind]))
        on(jnp.logical_not(less), lambda: drain(ref, nrow, sem.at[kind]))

    n_r[row] = n_s[...]
    m_r[row] = m_s[...]
    cf_r[:, own_half, :] = cot_ref[...]

    @pl.when(inside)
    def _():
        ct_r[row] = ct_s[mine]
        f_r[mine] = f_s[...]

    loads[6].wait()
    loads[7].wait()
    for c in range(proj):
        w32[c * (proj + PAD) : c * (proj + PAD) + proj, :] = w_ref[
            c * proj : (c + 1) * proj, :
        ].astype(F32)
    by_e = [w32[pl.ds(e, proj, stride=proj + PAD), :].astype(BF16) for e in range(proj)]
    w_c = jnp.concatenate(by_e, axis=1)

    def turned(k, b):
        return k // loc * loc + (k % loc - b) % loc

    eye = (iota((chan, chan), 0) == iota((chan, chan), 1)).astype(BF16)
    for b in range(loc):
        order = [turned(k, b) for k in range(proj)]
        turned_w = mm_t(
            eye, jnp.concatenate([w_ref[c * proj : (c + 1) * proj, :] for c in order], axis=0)
        ).astype(BF16)
        for t in range(proj // loc):
            wt_ref[b, t] = turned_w[:, t * 128 : (t + 1) * 128]

    def spread_left(gl, part):
        p = mm(gl[:, :proj], w_c).astype(BF16)
        for e in range(proj):
            for i in range(loc):
                at = (part * proj + e) * seq
                p2[i, at : at + seq, :] = p[
                    i * seq : (i + 1) * seq, e * chan : (e + 1) * chan
                ]

    def fold(outs, dst):
        lane_group = iota((1, 128), 1) >> (proj.bit_length() - 1)
        marks = [jnp.where(lane_group == p, 1.0, 0.0) for p in range(loc)]
        for t in range(proj // loc):
            part = [o[:, t * 128 : (t + 1) * 128] for o in outs]
            for k in range(loc):
                d = part[-k % loc] * marks[0]
                for p in range(1, loc):
                    d = d + part[(p - k) % loc] * marks[p]
                if k:
                    d = pltpu.roll(d, 128 - k * proj, 1)
                at = (t * loc + k) * (bres + PAD)
                dst[at : at + bres, :] = d

    def block(b):
        if isinstance(b, int):
            return pl.ds(b * bres, bres)
        return pl.ds(pl.multiple_of(b * bres, bres), bres)

    def outer_a(b):
        outs = []
        for i in range(loc):
            order = [turned(k, i) for k in range(proj)]
            outs.append(
                mm_t(cf_r[i, block(b), :], jnp.concatenate([by_e[e] for e in order], axis=0))
            )
        fold(outs, og_a)

    def outer_b(b):
        c32[...] = ct_r[pl.ds(b * br, br)].astype(F32).reshape(bres * loc, chan)
        fold(
            [
                mm(
                    c32[pl.ds(j, bres, stride=loc), :].astype(BF16),
                    jnp.concatenate([wt_ref[j, t] for t in range(proj // loc)], axis=1),
                )
                for j in range(loc)
            ],
            og_b,
        )

    def inverse(b):
        spot = (iota((bres, br), 0) >> lo == iota((bres, br), 1)).astype(BF16)
        own_lane = (iota((bres, 128), 0) & (loc - 1)) == (iota((bres, 128), 1) >> sq)
        total = None
        for k, own in enumerate((live_nat, live_other)):
            m = m_r[pl.ds(k * nrow + b * br, br)].reshape(br, 128).astype(BF16)
            m = jnp.where(own_lane, mm(spot, m), 0.0).astype(BF16)
            term = mm(m, jnp.concatenate([own] * (128 // seq), axis=0))
            total = term if total is None else total + term
        inv_ref[block(b), :] = 1.0 / jnp.maximum(total, 1.0)

    def operator(b, og, dst):
        for r in range(bres):
            dst[r * proj : (r + 1) * proj, :] = (
                og[pl.ds(r, proj, stride=bres + PAD), :] * inv_ref[pl.ds(b * bres + r, 1), :]
            ).astype(BF16)

    def grads(b, dst, k_ref, side, first):
        a = jnp.concatenate([n_r[b * br + r, side] for r in range(br)], axis=1)
        out = mm(a, k_ref[...])
        for i in range(loc):
            at = pl.ds(i, seq, stride=loc)
            part = out[:, i * proj : (i + 1) * proj]
            dst[at, :] = part if first else dst[at, :] + part

    spread_left(g, 0)
    partner(0).wait_recv()
    spread_left(g_r[:rows], 1)
    live_other = g_r[rows:]
    partner(1).wait_recv()
    if blocks == 1:
        outer_a(0)
    drain(m_r, 2 * nrow - 1, rsem.at[2])
    drain_some(ct_r, 3, rsem, inside)
    if blocks == 1:
        inverse(0)
        operator(0, og_a, k_a)
        outer_b(0)
        operator(0, og_b, k_b)
    drain(n_r, nrow - 1, rsem.at[4])
    drain_some(f_r, 5, rsem, inside)
    if blocks == 1:
        grads(0, lg_ref, k_a, 1, True)
        grads(0, rg_ref, k_b, 0, True)
    else:
        lg_ref[...] = jnp.zeros(lg_ref.shape, F32)
        rg_ref[...] = jnp.zeros(rg_ref.shape, F32)

        @pl.loop(0, blocks)
        def _(b):
            outer_a(b)
            outer_b(b)
            inverse(b)
            operator(b, og_a, k_a)
            operator(b, og_b, k_b)
            grads(b, lg_ref, k_a, 1, False)
            grads(b, rg_ref, k_b, 0, False)

    a32[...] = f_r[...].astype(F32).reshape(2 * half_res * tiles, 128)
    flat = jnp.concatenate(
        [
            a32[pl.ds(k * half_res * tiles + t, half_res, stride=tiles), :]
            for k in range(2)
            for t in range(tiles)
        ],
        axis=1,
    ).astype(BF16)
    mapped = mm(flat, jnp.concatenate([p2[i] for i in range(loc)], axis=1))
    bias = bias_ref[...]
    own_inv = inv_ref[own_half, :]
    for i in range(loc):
        inv = jnp.broadcast_to(own_inv[:, i * proj : i * proj + 1], (half_res, chan))
        pu_ref[i] = (mapped[:, i * chan : (i + 1) * chan] * inv + bias).astype(BF16)

    partner(0).wait_send()
    partner(1).wait_send()
    drain(m_r, 2 * nrow - 1, ssem.at[2])
    drain_some(ct_r, 3, ssem, inside)
    drain(n_r, nrow - 1, ssem.at[4])
    drain_some(f_r, 5, ssem, inside)


def finish(pu_in, lg_in, rg_in, pu_ref, lg_ref, rg_ref):
    pu_ref[...] = pu_in[...]
    lg_ref[...] = lg_in[...]
    rg_ref[...] = rg_in[...]


def per_device(nrow, x, am, rm, wl, wr, w, bias, cot):
    seq, loc, _ = x.shape
    proj = wl.shape[1]
    half_res, chan = cot.shape[1], cot.shape[2]
    res = nrow * loc
    tiles = proj * seq // 128
    fr = loc * tiles
    rows = loc * seq
    lanes = loc * proj
    per_half = half_res // loc
    bres = block_rows(nrow) * loc
    hbm = pl.BlockSpec(memory_space=pltpu.HBM)
    vm = pl.BlockSpec(memory_space=pltpu.VMEM)
    operands = (x, am.T, rm.reshape(1, loc), wl.T, wr.T, w, bias.reshape(1, chan), cot)
    held = [pltpu.with_memory_space_constraint(a, pltpu.HBM) for a in operands]
    pu, lg, rg = pl.pallas_call(
        functools.partial(kernel, nrow),
        out_shape=(
            jax.ShapeDtypeStruct(cot.shape, BF16),
            jax.ShapeDtypeStruct((rows, proj), F32),
            jax.ShapeDtypeStruct((rows, proj), F32),
        ),
        in_specs=[hbm] * 8,
        out_specs=(vm, vm, vm),
        scratch_shapes=[pltpu.VMEM(a.shape, a.dtype) for a in operands]
        + [
            pltpu.VMEM((rows + seq, 128), BF16),
            pltpu.VMEM((rows + seq, 128), BF16),
            pltpu.VMEM((2, seq, lanes), BF16),
            pltpu.VMEM((nrow, 2, seq, lanes), BF16),
            pltpu.VMEM((fr, 128), BF16),
            pltpu.VMEM((nrow, fr, 128), BF16),
            pltpu.VMEM((per_half, loc * loc, chan), BF16),
            pltpu.VMEM((nrow, loc * loc, chan), BF16),
            pltpu.VMEM((loc, res, chan), BF16),
            pltpu.VMEM((1, 128), F32),
            pltpu.VMEM((2 * nrow, 1, 128), F32),
            pltpu.VMEM((proj * (proj + PAD), chan), F32),
            pltpu.VMEM((2 * half_res * tiles, 128), F32),
            pltpu.VMEM((bres * loc, chan), F32),
            pltpu.VMEM((loc * half_res, chan), F32),
            pltpu.VMEM((res, lanes), F32),
            pltpu.VMEM((proj * (bres + PAD), lanes), F32),
            pltpu.VMEM((proj * (bres + PAD), lanes), F32),
            pltpu.VMEM((bres * proj, lanes), BF16),
            pltpu.VMEM((bres * proj, lanes), BF16),
            pltpu.VMEM((loc, proj // loc, chan, 128), BF16),
            pltpu.VMEM((loc, 2 * proj * seq, chan), BF16),
            pltpu.SemaphoreType.DMA((6,)),
            pltpu.SemaphoreType.DMA((6,)),
            pltpu.SemaphoreType.DMA((8,)),
        ],
        compiler_params=pltpu.CompilerParams(
            collective_id=0, has_side_effects=True, vmem_limit_bytes=GRANT
        ),
    )(*held)
    grads = jax.ShapeDtypeStruct((rows, proj), F32)
    pu, lg, rg = pl.pallas_call(
        finish,
        out_shape=(jax.ShapeDtypeStruct(cot.shape, BF16), grads, grads),
        in_specs=[vm] * 3,
        out_specs=(vm, vm, vm),
        compiler_params=pltpu.CompilerParams(vmem_limit_bytes=GRANT),
    )(pu, lg, rg)
    return pu, lg.reshape(seq, loc, proj), rg.reshape(seq, loc, proj)


def solution(mesh):
    placed = (
        P(("grp", "col"), "row", None),
        P(("grp", "col"), "row"),
        P(("grp", "row")),
        P(),
        P(),
        P(),
        P(),
        P(("grp", "row"), "col", None),
    )
    return jax.shard_map(
        functools.partial(per_device, mesh.shape["row"]),
        mesh=mesh,
        in_specs=placed,
        out_specs=(
            P(("grp", "row"), "col", None),
            P(("grp", "col"), "row", None),
            P(("grp", "col"), "row", None),
        ),
        check_vma=False,
    )
```
